256 devices in a mesh: sta: 64 (over z, y, core), win: 4 (over x).
Axes of the slice: x: 4, y: 4, z: 8, core: 2. Of those that a mesh axis runs over, the one named last changes fastest.
Arguments:
- spectra: bfloat16 [64, 448, 4096], P('win', 'sta'), may hold values from -6 to 6
- pair_bins: int32 [448, 3, 7], P('sta'), may hold values from 0 to 127
- owner_count: int32 [64], replicated, may hold values from 1 to 4, 128 in all
- bin_order: int32 [128], replicated, may hold values from 0 to 127, each once
Outputs:
- owned_stacks: float32 [256, 4096], P('sta', 'win')
The draws below stay inside these ranges and needn't reach their ends.
Inputs may be any that keep to these rules, and one draw needn't show every extreme that they name: Owner o holds owner_count[o] bins; the counts sum to 128 and the largest is exactly 4. `bin_order`: every bin appears exactly once.
All inputs are finite; a program needn't handle non-finite values.
Results may differ from the reference program's by a relative error of at most 0.0011.
Values may be sent and summed in bfloat16 or wider, within the bound.
No kernel may reach another device: no remote copies, remote signals or barrier semaphores. Data moves between devices by JAX's collectives and lax.ppermute only.
A program may use at most 128 MiB of HBM per device.

```python
import math
import jax
import jax.numpy as jnp
import numpy as np
from jax import lax

F = 2048
S_DEV = 7
W_DEV = 16
ROUNDS = 3
CAP = 4
STATIONS = 448
NWIN = 64
NBINS = 128
N_STA = 64
N_WIN = 4


def place_ends(result, key, smallest, largest):
    shape = result.shape
    place = [jax.random.randint(jax.random.fold_in(key, axis), (), 0, shape[axis]) for axis in range(len(shape))]
    result = result.at[tuple(place)].set(smallest)
    longest = shape.index(max(shape))
    place[longest] = (place[longest] + 1) % shape[longest]
    return result.at[tuple(place)].set(largest)


def block_levels(stream_key, dims, split, least, top_value):
    loudness, own = 1.0, jax.random.fold_in(stream_key, 6)
    for dim, blocks in split:
        draws = jnp.exp(jax.random.uniform(jax.random.fold_in(own, dim), (blocks,), jnp.float32, least / len(split), top_value / len(split)))
        loudness = loudness * jnp.repeat(draws, dims[dim] // blocks).reshape([-1 if axis == dim else 1 for axis in range(len(dims))])
    return loudness


def profile(count, total, limit, slope):
    weights = [(1 << 20) // math.isqrt(rank ** slope) + 1 for rank in range(2, count + 1)]
    surplus, given = total - limit - (count - 1), [1] * (count - 1)
    while surplus > 0:
        movable = [i for i in range(count - 1) if given[i] < limit]
        whole, remaining = sum([weights[i] for i in movable]), surplus
        for i in movable:
            extra = min(limit - given[i], max(1, remaining * weights[i] // whole), surplus)
            given[i] = given[i] + extra
            surplus = surplus - extra
    return np.array([limit] + given)


def uneven_parts(key, amount, total, limit, slope):
    if amount == 2:
        one = jax.random.randint(key, (), max(1, total - limit), min(limit, total - 1) + 1)
        return jnp.stack([one, total - one])
    tallies = jnp.asarray(profile(amount, total, limit, slope), jnp.int32)
    twos = (amount - 1) // 2
    source_of, receiver = tallies[1:1 + 2 * twos:2], tallies[2:2 + 2 * twos:2]
    room = jnp.minimum(source_of - 1, limit - receiver)
    passed = jax.random.randint(jax.random.fold_in(key, 1), (twos,), 0, 1 << 20) % (room + 1)
    tallies = tallies.at[1:1 + 2 * twos:2].set(source_of - passed).at[2:2 + 2 * twos:2].set(receiver + passed)
    return tallies[jax.random.permutation(jax.random.fold_in(key, 2), amount)]


def normal_values(own_key, shape, scale, limit, cuts=(), kind=jnp.bfloat16):
    factor_of = block_levels(own_key, shape, cuts, -0.22, 0.18) if cuts else 1.0
    entries = jax.random.normal(own_key, shape, jnp.float32) * scale * factor_of
    return jnp.minimum(jnp.maximum(entries, -limit), limit).astype(kind)


def setup_inputs(seed: int = 0) -> dict:
    streams_of = jax.random.split(jax.random.key(seed), 5)
    return {
        "spectra": normal_values(streams_of[0], (NWIN, STATIONS, 2 * F), 1.0, 6.0, ((0, 4), (1, 64))),
        "pair_bins": place_ends(jax.random.randint(streams_of[1], (STATIONS, ROUNDS, S_DEV), 0, NBINS), jax.random.fold_in(streams_of[1], 1), 0, NBINS - 1).astype(jnp.int32),
        "owner_count": uneven_parts(streams_of[2], N_STA, NBINS, CAP, 2).astype(jnp.int32),
        "bin_order": jax.random.permutation(streams_of[3], NBINS).astype(jnp.int32),
    }


def cross_all(own, other):
    width = own.shape[-1] // 2
    own_re, own_im = own[..., :width], own[..., width:]
    other_re, other_im = other[..., :width], other[..., width:]
    form = "gwsf,gwtf->gstf"
    real = jnp.einsum(form, own_re, other_re, precision=lax.Precision.HIGHEST) + jnp.einsum(form, own_im, other_im, precision=lax.Precision.HIGHEST)
    imag = jnp.einsum(form, own_im, other_re, precision=lax.Precision.HIGHEST) - jnp.einsum(form, own_re, other_im, precision=lax.Precision.HIGHEST)
    return jnp.concatenate([real, imag], axis=-1)


def reference(spectra, pair_bins, owner_count, bin_order):
    shaped = spectra.reshape(N_WIN, W_DEV, N_STA, S_DEV, 2 * F)
    bins_shaped = pair_bins.reshape(N_STA, S_DEV, ROUNDS, S_DEV)

    def per_block(totals, block):
        own = lax.dynamic_index_in_dim(shaped, block, 2, keepdims=False).astype(jnp.float32)
        labels_all = lax.dynamic_index_in_dim(bins_shaped, block, 0, keepdims=False)
        for offset in range(ROUNDS):
            partner = ((block - offset) % N_STA).astype(jnp.int32)
            other = lax.dynamic_index_in_dim(shaped, partner, 2, keepdims=False).astype(jnp.float32)
            crossed = cross_all(own, other)
            rounded = lax.optimization_barrier(crossed.astype(jnp.bfloat16)).astype(jnp.float32)
            labels = jnp.broadcast_to(labels_all[:, offset, :], (N_WIN, S_DEV, S_DEV)).reshape(-1)
            totals = totals + jax.ops.segment_sum(rounded.reshape(-1, 2 * F), labels, num_segments=NBINS)
        return totals, None

    totals, _ = lax.scan(per_block, jnp.zeros((NBINS, 2 * F), jnp.float32), jnp.arange(N_STA, dtype=jnp.int32))
    starts = (jnp.cumsum(owner_count) - owner_count).astype(jnp.int32)
    ranks = jnp.arange(CAP, dtype=jnp.int32)
    positions = jnp.clip(starts[:, None] + ranks[None, :], 0, NBINS - 1).astype(jnp.int32)
    valid = ranks[None, :] < owner_count[:, None]
    chosen = bin_order[positions]
    stacks = jnp.where(valid[..., None], totals[chosen], jnp.float32(0.0))
    return stacks.reshape(N_STA * CAP, 2 * F) * jnp.float32(1.0 / NWIN)
```

```python
import jax
import jax.numpy as jnp
from jax import lax
from jax.experimental import pallas as pl
from jax.experimental.pallas import tpu as pltpu
from jax.sharding import Mesh, PartitionSpec as P

PLANE = 8
STA = 7
WIN = 16
NG = 4
ROUNDS = 3
CAP = 4
ROWS = STA * WIN
MSG = ROWS + 8
LANES = 128
CHUNK = 32
KI = 256
F32 = jnp.float32
BF16 = jnp.bfloat16


def lane_iota(shape):
    return lax.broadcasted_iota(jnp.int32, shape, len(shape) - 1)


def chunk_transpose(tiles):
    lane = lane_iota(tiles[0].shape)
    low = lane < 64
    even = (lane % 64) < CHUNK
    axis = tiles[0].ndim - 1

    def half(a, b):
        return jnp.where(low, a, pltpu.roll(b, 64, axis)), jnp.where(low, pltpu.roll(a, 64, axis), b)

    def quarter(a, b):
        return jnp.where(even, a, pltpu.roll(b, CHUNK, axis)), jnp.where(even, pltpu.roll(a, LANES - CHUNK, axis), b)

    u0, u2 = half(tiles[0], tiles[2])
    u1, u3 = half(tiles[1], tiles[3])
    v0, v1 = quarter(u0, u1)
    v2, v3 = quarter(u2, u3)
    return v0, v1, v2, v3


def pack_kernel(x_ref, bins_ref, out_ref):
    lane8 = lax.broadcasted_iota(jnp.int32, (STA, LANES), 1)
    row8 = lax.broadcasted_iota(jnp.int32, (STA, LANES), 0)
    labels = jnp.zeros((STA, LANES), F32)
    for r in range(ROUNDS):
        place = jnp.where(lane8 == row8 + 8 * r, 1.0, 0.0).astype(F32)
        labels = labels + jnp.dot(bins_ref[r].astype(F32), place, preferred_element_type=F32)
    labels = jnp.concatenate([labels, jnp.zeros((1, LANES), F32)], axis=0).astype(BF16)

    def step(q, carry):
        col = pl.multiple_of(q * LANES, LANES)
        for s in range(STA):
            tiles = [x_ref[s, :, pl.ds(n * 1024 + col, LANES)].astype(F32) for n in range(4)]
            for m, tile in enumerate(chunk_transpose(tiles)):
                out_ref[4 * q + m, s * WIN:(s + 1) * WIN, :] = tile.astype(BF16)
        for m in range(4):
            out_ref[4 * q + m, ROWS:MSG, :] = labels
        return carry

    lax.fori_loop(0, 8, step, 0)


def slot_bins(count_ref, order_ref):
    row = lax.broadcasted_iota(jnp.int32, (64, 64), 0)
    lane = lax.broadcasted_iota(jnp.int32, (64, 64), 1)
    counts = jnp.broadcast_to(count_ref[...].astype(F32), (64, 64))
    start = jnp.sum(jnp.where(lane < row, counts, 0.0), axis=1, keepdims=True)
    count = jnp.sum(jnp.where(lane == row, counts, 0.0), axis=1, keepdims=True)
    lane = lax.broadcasted_iota(jnp.int32, (64, LANES), 1).astype(F32)
    order = jnp.broadcast_to(order_ref[...].astype(F32), (64, LANES))
    out = []
    for k in range(CAP):
        chosen = jnp.sum(jnp.where(lane == start + float(k), order, 0.0), axis=1, keepdims=True)
        out.append(jnp.where(count > float(k), chosen, -1.0))
    return out


def cross_kernel(own_ref, halo_ref, count_ref, order_ref, out_ref, c_ref, cs_ref, f_ref, x_ref, hot_ref):
    lane = lane_iota((8, LANES))
    low = lane < 64
    zero = jnp.zeros((8, LANES), F32)

    spread = jnp.where(lax.broadcasted_iota(jnp.int32, (LANES, KI), 1) // 8
                       == lax.broadcasted_iota(jnp.int32, (LANES, KI), 0), 1.0, 0.0)
    qmod = lax.broadcasted_iota(jnp.int32, (8, KI), 1) % 8
    labels = jnp.zeros((8, KI), F32)
    for b in range(PLANE):
        wide = jnp.dot(own_ref[b * NG, ROWS:MSG, :].astype(F32), spread, preferred_element_type=F32)
        labels = labels + jnp.where(qmod == b, wide, 0.0)
    bins = [jnp.broadcast_to(v, (64, KI)) for v in slot_bins(count_ref, order_ref)]
    for i in range(STA):
        row = jnp.broadcast_to(labels[i:i + 1, :], (64, KI))
        for k in range(CAP):
            hot_ref[k * 64:(k + 1) * 64, i * KI:(i + 1) * KI] = jnp.where(bins[k] == row, 1.0, 0.0).astype(BF16)

    for i in range(STA):
        for r in range(ROUNDS):
            f_ref[i, (r * 8 + 7) * 8:(r * 8 + 8) * 8, :] = zero
        for n in range(8):
            f_ref[i, (24 + n) * 8:(25 + n) * 8, :] = zero

    def per_shard(g, carry):
        sign = jnp.where(lane_iota((ROWS, LANES)) < 64, -1.0, 1.0).astype(F32)
        for bb in range(PLANE + 2):
            if bb < 2:
                piece = halo_ref[bb * NG + g, 0:ROWS, :]
            else:
                piece = own_ref[(bb - 2) * NG + g, 0:ROWS, :]
            piece = piece.astype(F32)
            turned = pltpu.roll(piece, 64, 1) * sign
            for s in range(STA):
                c_ref[s, bb * WIN:(bb + 1) * WIN, :] = piece[s * WIN:(s + 1) * WIN, :]
                cs_ref[s, bb * WIN:(bb + 1) * WIN, :] = turned[s * WIN:(s + 1) * WIN, :]

        def put(i, r, j, value):
            f_ref[i, (r * 8 + j) * 8:(r * 8 + j + 1) * 8, :] = value

        def joined(p, q):
            return jnp.where(low, p, q) + pltpu.roll(jnp.where(low, q, p), 64, 1)

        def group(pairs, r):
            own = sorted({i for i, _ in pairs})
            other = sorted({j for _, j in pairs})
            acc_p, acc_q = {}, {}
            for w in range(WIN):
                a = {i: c_ref[i, pl.ds(2 * WIN + w, 8, stride=WIN), :] for i in own}
                for j in other:
                    c = c_ref[j, pl.ds((2 - r) * WIN + w, 8, stride=WIN), :]
                    d = cs_ref[j, pl.ds((2 - r) * WIN + w, 8, stride=WIN), :]
                    for i in own:
                        if (i, j) not in pairs:
                            continue
                        p = a[i] * c
                        acc_p[i, j] = p if w == 0 else acc_p[i, j] + p
                        if r == 0 and i == j:
                            continue
                        q = a[i] * d
                        acc_q[i, j] = q if w == 0 else acc_q[i, j] + q
            for i, j in pairs:
                value = joined(acc_p[i, j], acc_q.get((i, j), zero))
                put(i, r, j, value)
                if r == 0 and i != j:
                    put(j, r, i, jnp.where(low, value, -value))

        for own in ((0, 1), (2, 3), (4, 5, 6)):
            group([(i, j) for i in own for j in range(i, STA)], 0)
        for r in (1, 2):
            for own in ((0, 1), (2, 3), (4, 5), (6,)):
                group([(i, j) for i in own for j in range(STA)], r)
        for i in range(STA):
            x_ref[i * KI:(i + 1) * KI, pl.ds(pl.multiple_of(g * LANES, LANES), LANES)] = f_ref[i].astype(BF16)
        return carry

    lax.fori_loop(0, NG, per_shard, 0)
    total = jnp.dot(hot_ref[...], x_ref[...], preferred_element_type=F32)
    total = (total[:, 0:128] + total[:, 128:256]) + (total[:, 256:384] + total[:, 384:512])
    for w, tile in enumerate(chunk_transpose([total[k * 64:(k + 1) * 64, :] for k in range(CAP)])):
        out_ref[pl.ds(w, 64, stride=4), :] = tile


def finish_kernel(in_ref, out_ref, s_ref):
    total = in_ref[0]
    for z in range(1, 8):
        total = total + in_ref[z]
    s_ref[...] = total * (1.0 / 64.0)
    tiles = chunk_transpose([s_ref[pl.ds(m, 8, stride=4), :] for m in range(4)])
    for k in range(CAP):
        for t in range(8):
            out_ref[k:k + 1, t * LANES:(t + 1) * LANES] = tiles[k][t:t + 1, :]


def on_device(spectra, pair_bins, owner_count, bin_order):
    vmem = pl.BlockSpec(memory_space=pltpu.VMEM)
    packed = pl.pallas_call(
        pack_kernel,
        out_shape=jax.ShapeDtypeStruct((32, MSG, LANES), BF16),
        in_specs=[vmem, vmem],
        out_specs=vmem,
        name="pack",
    )(jnp.transpose(spectra, (1, 0, 2)), jnp.transpose(pair_bins, (1, 0, 2)))
    own = lax.all_to_all(packed, ("y", "c", "win"), 0, 0)
    count = lax.axis_size("z")
    halo = lax.ppermute(own[24:32], "z", [(i, (i + 1) % count) for i in range(count)])
    send = pl.pallas_call(
        cross_kernel,
        out_shape=jax.ShapeDtypeStruct((256, LANES), F32),
        in_specs=[vmem] * 4,
        out_specs=vmem,
        scratch_shapes=[
            pltpu.VMEM((STA, (PLANE + 2) * WIN, LANES), F32),
            pltpu.VMEM((STA, (PLANE + 2) * WIN, LANES), F32),
            pltpu.VMEM((STA, KI, LANES), F32),
            pltpu.VMEM((STA * KI, NG * LANES), BF16),
            pltpu.VMEM((256, STA * KI), BF16),
        ],
        name="cross",
    )(own, halo, owner_count.reshape(1, -1), bin_order.reshape(1, -1))
    got = lax.all_to_all(send.reshape(256, 1, LANES), ("z", "y", "c", "win"), 0, 0)
    return pl.pallas_call(
        finish_kernel,
        out_shape=jax.ShapeDtypeStruct((CAP, 1024), F32),
        in_specs=[vmem],
        out_specs=vmem,
        scratch_shapes=[pltpu.VMEM((32, LANES), F32)],
        name="finish",
    )(got.reshape(8, 32, LANES))


def solution(mesh):
    fine = Mesh(mesh.devices.reshape(8, 4, 2, 4), ("z", "y", "c", "win"))
    sta = ("z", "y", "c")
    return jax.shard_map(
        on_device,
        mesh=fine,
        in_specs=(P("win", sta, None), P(sta, None, None), P(), P()),
        out_specs=P(sta, "win"),
        check_vma=False,
    )
```

```python
import jax
import jax.numpy as jnp
from jax import lax
from jax.experimental import pallas as pl
from jax.experimental.pallas import tpu as pltpu
from jax.sharding import Mesh, PartitionSpec as P

PLANE = 8
STA = 7
WIN = 16
NG = 4
ROUNDS = 3
CAP = 4
ROWS = STA * WIN
MSG = ROWS + 8
PITCH = WIN + 1
LANES = 128
CHUNK = 32
KI = 256
F32 = jnp.float32
BF16 = jnp.bfloat16


def lane_iota(shape):
    return lax.broadcasted_iota(jnp.int32, shape, len(shape) - 1)


def chunk_transpose(tiles):
    lane = lane_iota(tiles[0].shape)
    low = lane < 64
    even = (lane % 64) < CHUNK
    axis = tiles[0].ndim - 1

    def half(a, b):
        return jnp.where(low, a, pltpu.roll(b, 64, axis)), jnp.where(low, pltpu.roll(a, 64, axis), b)

    def quarter(a, b):
        return jnp.where(even, a, pltpu.roll(b, CHUNK, axis)), jnp.where(even, pltpu.roll(a, LANES - CHUNK, axis), b)

    u0, u2 = half(tiles[0], tiles[2])
    u1, u3 = half(tiles[1], tiles[3])
    v0, v1 = quarter(u0, u1)
    v2, v3 = quarter(u2, u3)
    return v0, v1, v2, v3


def pack_kernel(x_ref, bins_ref, out_ref):
    lane8 = lax.broadcasted_iota(jnp.int32, (STA, LANES), 1)
    row8 = lax.broadcasted_iota(jnp.int32, (STA, LANES), 0)
    labels = jnp.zeros((STA, LANES), F32)
    for r in range(ROUNDS):
        place = jnp.where(lane8 == row8 + 8 * r, 1.0, 0.0).astype(F32)
        labels = labels + jnp.dot(bins_ref[r].astype(F32), place, preferred_element_type=F32)
    labels = jnp.concatenate([labels, jnp.zeros((1, LANES), F32)], axis=0).astype(BF16)

    def step(q, carry):
        col = pl.multiple_of(q * LANES, LANES)
        for s in range(STA):
            tiles = [x_ref[s, :, pl.ds(n * 1024 + col, LANES)] for n in range(4)]
            for m, tile in enumerate(chunk_transpose(tiles)):
                out_ref[4 * q + m, s * WIN:(s + 1) * WIN, :] = tile
        for m in range(4):
            out_ref[4 * q + m, ROWS:MSG, :] = labels
        return carry

    lax.fori_loop(0, 8, step, 0)


def slot_bins(count_ref, order_ref):
    row = lax.broadcasted_iota(jnp.int32, (64, 64), 0)
    lane = lax.broadcasted_iota(jnp.int32, (64, 64), 1)
    counts = jnp.broadcast_to(count_ref[...].astype(F32), (64, 64))
    start = jnp.sum(jnp.where(lane < row, counts, 0.0), axis=1, keepdims=True)
    count = jnp.sum(jnp.where(lane == row, counts, 0.0), axis=1, keepdims=True)
    lane = lax.broadcasted_iota(jnp.int32, (64, LANES), 1).astype(F32)
    order = jnp.broadcast_to(order_ref[...].astype(F32), (64, LANES))
    out = []
    for k in range(CAP):
        chosen = jnp.sum(jnp.where(lane == start + float(k), order, 0.0), axis=1, keepdims=True)
        out.append(jnp.where(count > float(k), chosen, -1.0))
    return out


def cross_kernel(own_ref, halo_ref, count_ref, order_ref, out_ref, c_ref, t_ref, f_ref, x_ref, hot_ref):
    lane = lane_iota((8, LANES))
    low = lane < 64
    zero = jnp.zeros((8, LANES), F32)

    spread = jnp.where(lax.broadcasted_iota(jnp.int32, (LANES, KI), 1) // 8
                       == lax.broadcasted_iota(jnp.int32, (LANES, KI), 0), 1.0, 0.0)
    qmod = lax.broadcasted_iota(jnp.int32, (8, KI), 1) % 8
    labels = jnp.zeros((8, KI), F32)
    for b in range(PLANE):
        wide = jnp.dot(own_ref[b * NG, ROWS:MSG, :].astype(F32), spread, preferred_element_type=F32)
        labels = labels + jnp.where(qmod == b, wide, 0.0)
    bins = [jnp.broadcast_to(v, (64, KI)) for v in slot_bins(count_ref, order_ref)]
    for i in range(STA):
        row = jnp.broadcast_to(labels[i:i + 1, :], (64, KI))
        for k in range(CAP):
            hot_ref[k * 64:(k + 1) * 64, i * KI:(i + 1) * KI] = jnp.where(bins[k] == row, 1.0, 0.0).astype(BF16)

    for i in range(STA):
        f_ref[i, STA * 8:(STA + 1) * 8, :] = zero
        x_ref[i * KI + ROUNDS * 64:(i + 1) * KI, :] = jnp.zeros((64, NG * LANES), BF16)

    def per_shard(g, carry):
        sign = jnp.where(lane_iota((ROWS, LANES)) < 64, 1.0, -1.0).astype(F32)
        for bb in range(PLANE + 2):
            if bb < 2:
                piece = halo_ref[bb * NG + g, 0:ROWS, :].astype(F32)
            else:
                piece = own_ref[(bb - 2) * NG + g, 0:ROWS, :].astype(F32)
                turned = pltpu.roll(piece, 64, 1) * sign
            for s in range(STA):
                rows = slice(s * WIN, (s + 1) * WIN)
                c_ref[s, bb * PITCH:bb * PITCH + WIN, :] = piece[rows]
                if bb >= 2:
                    t_ref[s, (bb - 2) * PITCH:(bb - 2) * PITCH + WIN, :] = turned[rows]

        lanes = pl.ds(pl.multiple_of(g * LANES, LANES), LANES)

        def joined(p, q):
            return jnp.where(low, p, q) + pltpu.roll(jnp.where(low, q, p), 64, 1)

        def row_of(i, r, others):
            p, q = {}, {}
            for w in range(WIN):
                a = c_ref[i, pl.ds(2 * PITCH + w, 8, stride=PITCH), :]
                t = t_ref[i, pl.ds(w, 8, stride=PITCH), :]
                for j in others:
                    if r == 0 and j == i:
                        v = a * a
                        p[j] = v if w == 0 else p[j] + v
                        continue
                    c = c_ref[j, pl.ds((2 - r) * PITCH + w, 8, stride=PITCH), :]
                    v = a * c
                    p[j] = v if w == 0 else p[j] + v
                    v = t * c
                    q[j] = v if w == 0 else q[j] + v
            return {j: joined(p[j], q.get(j, zero)) for j in others}

        for i in range(STA):
            for j, value in row_of(i, 0, list(range(i, STA))).items():
                f_ref[i, j * 8:(j + 1) * 8, :] = value
                if j != i:
                    f_ref[j, i * 8:(i + 1) * 8, :] = jnp.where(low, value, -value)
            for r in (1, 2):
                values = row_of(i, r, list(range(STA)))
                values[STA] = zero
                for j in range(0, 8, 2):
                    pair = jnp.concatenate([values[j], values[j + 1]], axis=0).astype(BF16)
                    base = i * KI + (r * 8 + j) * 8
                    x_ref[base:base + 16, lanes] = pair
        for i in range(STA):
            x_ref[i * KI:i * KI + 64, lanes] = f_ref[i].astype(BF16)
        return carry

    lax.fori_loop(0, NG, per_shard, 0)
    total = jnp.dot(hot_ref[...], x_ref[...], preferred_element_type=F32)
    total = (total[:, 0:128] + total[:, 128:256]) + (total[:, 256:384] + total[:, 384:512])
    for w, tile in enumerate(chunk_transpose([total[k * 64:(k + 1) * 64, :] for k in range(CAP)])):
        out_ref[pl.ds(w, 64, stride=4), :] = tile


def finish_kernel(in_ref, out_ref, s_ref):
    total = in_ref[0]
    for z in range(1, 8):
        total = total + in_ref[z]
    s_ref[...] = total * (1.0 / 64.0)
    tiles = chunk_transpose([s_ref[pl.ds(m, 8, stride=4), :] for m in range(4)])
    for k in range(CAP):
        for t in range(8):
            out_ref[k:k + 1, t * LANES:(t + 1) * LANES] = tiles[k][t:t + 1, :]


def on_device(spectra, pair_bins, owner_count, bin_order):
    vmem = pl.BlockSpec(memory_space=pltpu.VMEM)
    packed = pl.pallas_call(
        pack_kernel,
        out_shape=jax.ShapeDtypeStruct((32, MSG, LANES), BF16),
        in_specs=[vmem, vmem],
        out_specs=vmem,
        name="pack",
    )(jnp.transpose(spectra, (1, 0, 2)), jnp.transpose(pair_bins, (1, 0, 2)))
    own = lax.all_to_all(packed, ("y", "c", "win"), 0, 0)
    count = lax.axis_size("z")
    halo = lax.ppermute(own[24:32], "z", [(i, (i + 1) % count) for i in range(count)])
    send = pl.pallas_call(
        cross_kernel,
        out_shape=jax.ShapeDtypeStruct((256, LANES), F32),
        in_specs=[vmem] * 4,
        out_specs=vmem,
        scratch_shapes=[
            pltpu.VMEM((STA, 176, LANES), F32),
            pltpu.VMEM((STA, 144, LANES), F32),
            pltpu.VMEM((STA, 64, LANES), F32),
            pltpu.VMEM((STA * KI, NG * LANES), BF16),
            pltpu.VMEM((256, STA * KI), BF16),
        ],
        name="cross",
    )(own, halo, owner_count.reshape(1, -1), bin_order.reshape(1, -1))
    got = lax.all_to_all(send.reshape(256, 1, LANES), ("z", "y", "c", "win"), 0, 0)
    return pl.pallas_call(
        finish_kernel,
        out_shape=jax.ShapeDtypeStruct((CAP, 1024), F32),
        in_specs=[vmem],
        out_specs=vmem,
        scratch_shapes=[pltpu.VMEM((32, LANES), F32)],
        name="finish",
    )(got.reshape(8, 32, LANES))


def solution(mesh):
    fine = Mesh(mesh.devices.reshape(8, 4, 2, 4), ("z", "y", "c", "win"))
    sta = ("z", "y", "c")
    return jax.shard_map(
        on_device,
        mesh=fine,
        in_specs=(P("win", sta, None), P(sta, None, None), P(), P()),
        out_specs=P(sta, "win"),
        check_vma=False,
    )
```

```python
import jax
import jax.numpy as jnp
from jax import lax
from jax.experimental import pallas as pl
from jax.experimental.pallas import tpu as pltpu
from jax.sharding import Mesh, PartitionSpec as P

PLANE = 8
STA = 7
WIN = 16
NG = 4
ROUNDS = 3
CAP = 4
ROWS = STA * WIN
MSG = ROWS + 8
PITCH = WIN + 1
LANES = 128
CHUNK = 32
KI = 256
F32 = jnp.float32
BF16 = jnp.bfloat16


def lane_iota(shape):
    return lax.broadcasted_iota(jnp.int32, shape, len(shape) - 1)


def chunk_transpose(tiles):
    lane = lane_iota(tiles[0].shape)
    low = lane < 64
    even = (lane % 64) < CHUNK
    axis = tiles[0].ndim - 1

    def half(a, b):
        return jnp.where(low, a, pltpu.roll(b, 64, axis)), jnp.where(low, pltpu.roll(a, 64, axis), b)

    def quarter(a, b):
        return jnp.where(even, a, pltpu.roll(b, CHUNK, axis)), jnp.where(even, pltpu.roll(a, LANES - CHUNK, axis), b)

    u0, u2 = half(tiles[0], tiles[2])
    u1, u3 = half(tiles[1], tiles[3])
    v0, v1 = quarter(u0, u1)
    v2, v3 = quarter(u2, u3)
    return v0, v1, v2, v3


def pack_kernel(x_hbm, bins_ref, out_ref, x_ref, sems):
    def station(s):
        return pltpu.make_async_copy(x_hbm.at[s], x_ref.at[s], sems.at[s])

    for s in range(STA):
        station(s).start()
    lane8 = lax.broadcasted_iota(jnp.int32, (STA, LANES), 1)
    row8 = lax.broadcasted_iota(jnp.int32, (STA, LANES), 0)
    labels = jnp.zeros((STA, LANES), F32)
    for r in range(ROUNDS):
        place = jnp.where(lane8 == row8 + 8 * r, 1.0, 0.0).astype(F32)
        labels = labels + jnp.dot(bins_ref[r].astype(F32), place, preferred_element_type=F32)
    labels = jnp.concatenate([labels, jnp.zeros((1, LANES), F32)], axis=0).astype(BF16)

    for d in range(32):
        out_ref[d, ROWS:MSG, :] = labels

    def step(s, carry):
        station(s).wait()
        rows = pl.ds(pl.multiple_of(s * WIN, WIN), WIN)
        for q in range(8):
            tiles = [x_ref[s, :, n * 1024 + q * LANES:n * 1024 + (q + 1) * LANES] for n in range(4)]
            for m, tile in enumerate(chunk_transpose(tiles)):
                out_ref[4 * q + m, rows, :] = tile
        return carry

    lax.fori_loop(0, STA, step, 0)


def slot_bins(count_ref, order_ref):
    row = lax.broadcasted_iota(jnp.int32, (64, 64), 0)
    lane = lax.broadcasted_iota(jnp.int32, (64, 64), 1)
    counts = jnp.broadcast_to(count_ref[...].astype(F32), (64, 64))
    start = jnp.sum(jnp.where(lane < row, counts, 0.0), axis=1, keepdims=True)
    count = jnp.sum(jnp.where(lane == row, counts, 0.0), axis=1, keepdims=True)
    lane = lax.broadcasted_iota(jnp.int32, (64, LANES), 1).astype(F32)
    order = jnp.broadcast_to(order_ref[...].astype(F32), (64, LANES))
    out = []
    for k in range(CAP):
        chosen = jnp.sum(jnp.where(lane == start + float(k), order, 0.0), axis=1, keepdims=True)
        out.append(jnp.where(count > float(k), chosen, -1.0))
    return out


def joined(p, q):
    low = lane_iota(p.shape) < 64
    return jnp.where(low, p, q) + pltpu.roll(jnp.where(low, q, p), 64, 1)


def cross_kernel(own_ref, count_ref, order_ref, out_ref, edge_hot_ref, c_ref, t_ref, f_ref, x_ref, hot_ref):
    lane = lane_iota((8, LANES))
    low = lane < 64
    zero = jnp.zeros((8, LANES), F32)

    spread = jnp.where(lax.broadcasted_iota(jnp.int32, (LANES, KI), 1) // 8
                       == lax.broadcasted_iota(jnp.int32, (LANES, KI), 0), 1.0, 0.0)
    lane_q = lane_iota((8, KI))
    qmod = lane_q % 8
    labels = jnp.zeros((8, KI), F32)
    for b in range(PLANE):
        wide = jnp.dot(own_ref[b * NG, ROWS:MSG, :].astype(F32), spread, preferred_element_type=F32)
        labels = labels + jnp.where(qmod == b, wide, 0.0)
    labels = jnp.where(lane_q // 64 > qmod, -2.0, labels)

    col = lane_iota((LANES, LANES))
    row = lax.broadcasted_iota(jnp.int32, (LANES, LANES), 0)
    variant, half, station = col // 64, (col % 8) // 4, (col // 8) % 8
    first = jnp.where((variant == 0) & (row == (1 + half) * 8 + station), 1.0, 0.0).astype(F32)
    second = jnp.where((variant == 1) & (row == 2 * 8 + station), 1.0, 0.0).astype(F32)
    edge = jnp.dot(own_ref[0, ROWS:MSG, :].astype(F32), first, preferred_element_type=F32)
    edge = edge + jnp.dot(own_ref[NG, ROWS:MSG, :].astype(F32), second, preferred_element_type=F32)
    lane_e = lane_iota((8, LANES))
    edge = jnp.where((lane_e >= 64) & (lane_e % 8 >= 4), -2.0, edge)

    bins = [jnp.broadcast_to(v, (64, KI)) for v in slot_bins(count_ref, order_ref)]
    for i in range(STA):
        row = jnp.broadcast_to(labels[i:i + 1, :], (64, KI))
        edge_row = jnp.broadcast_to(edge[i:i + 1, :], (64, LANES))
        for k in range(CAP):
            rows = slice(k * 64, (k + 1) * 64)
            hot_ref[rows, i * KI:(i + 1) * KI] = jnp.where(bins[k] == row, 1.0, 0.0).astype(BF16)
            edge_hot_ref[rows, i * LANES:(i + 1) * LANES] = jnp.where(
                bins[k][:, :LANES] == edge_row, 1.0, 0.0).astype(BF16)

    for i in range(STA):
        f_ref[i, STA * 8:(STA + 1) * 8, :] = zero
        x_ref[i * KI + ROUNDS * 64:(i + 1) * KI, :] = jnp.zeros((64, NG * LANES), BF16)
        c_ref[i, 0:2 * PITCH, :] = jnp.zeros((2 * PITCH, LANES), F32)

    def per_shard(g, carry):
        sign = jnp.where(lane_iota((ROWS, LANES)) < 64, 1.0, -1.0).astype(F32)
        for b in range(PLANE):
            piece = own_ref[b * NG + g, 0:ROWS, :].astype(F32)
            turned = pltpu.roll(piece, 64, 1) * sign
            for s in range(STA):
                rows = slice(s * WIN, (s + 1) * WIN)
                c_ref[s, (b + 2) * PITCH:(b + 2) * PITCH + WIN, :] = piece[rows]
                t_ref[s, b * PITCH:b * PITCH + WIN, :] = turned[rows]

        lanes = pl.ds(pl.multiple_of(g * LANES, LANES), LANES)

        def row_of(i, r, others):
            p, q = {}, {}
            for w in range(WIN):
                a = c_ref[i, pl.ds(2 * PITCH + w, 8, stride=PITCH), :]
                t = t_ref[i, pl.ds(w, 8, stride=PITCH), :]
                for j in others:
                    if r == 0 and j == i:
                        v = a * a
                        p[j] = v if w == 0 else p[j] + v
                        continue
                    c = c_ref[j, pl.ds((2 - r) * PITCH + w, 8, stride=PITCH), :]
                    v = a * c
                    p[j] = v if w == 0 else p[j] + v
                    v = t * c
                    q[j] = v if w == 0 else q[j] + v
            return {j: joined(p[j], q.get(j, zero)) for j in others}

        for i in range(STA):
            for j, value in row_of(i, 0, list(range(i, STA))).items():
                f_ref[i, j * 8:(j + 1) * 8, :] = value
                if j != i:
                    f_ref[j, i * 8:(i + 1) * 8, :] = jnp.where(low, value, -value)
            for r in (1, 2):
                values = row_of(i, r, list(range(STA)))
                values[STA] = zero
                for j in range(0, 8, 2):
                    pair = jnp.concatenate([values[j], values[j + 1]], axis=0).astype(BF16)
                    base = i * KI + (r * 8 + j) * 8
                    x_ref[base:base + 16, lanes] = pair
        for i in range(STA):
            x_ref[i * KI:i * KI + 64, lanes] = f_ref[i].astype(BF16)
        return carry

    lax.fori_loop(0, NG, per_shard, 0)
    total = jnp.dot(hot_ref[...], x_ref[...], preferred_element_type=F32)
    out_ref[...] = (total[:, 0:128] + total[:, 128:256]) + (total[:, 256:384] + total[:, 384:512])


def edge_kernel(own_ref, halo_ref, part_ref, hot_ref, out_ref, a_ref, t_ref, c_ref, x_ref):
    sign = jnp.where(lane_iota((ROWS, LANES)) < 64, 1.0, -1.0).astype(F32)
    zero = jnp.zeros((8, LANES), F32)
    for g in range(NG):
        for slot, (ref, index) in enumerate(((own_ref, g), (own_ref, NG + g), (halo_ref, NG + g), (halo_ref, g))):
            piece = ref[index, 0:ROWS, :].astype(F32)
            for s in range(STA):
                rows = piece[s * WIN:(s + 1) * WIN]
                if slot >= 2:
                    base = ((slot - 2) * 4 + g) * PITCH
                    c_ref[s, base:base + WIN, :] = rows
                else:
                    for half in range(2):
                        base = (slot * 8 + half * 4 + g) * PITCH
                        a_ref[s, base:base + WIN, :] = rows
            if slot < 2:
                turned = pltpu.roll(piece, 64, 1) * sign
                for s in range(STA):
                    for half in range(2):
                        base = (slot * 8 + half * 4 + g) * PITCH
                        t_ref[s, base:base + WIN, :] = turned[s * WIN:(s + 1) * WIN]

    def per_station(i, carry):
        for variant in range(2):
            p, q = {}, {}
            for w in range(WIN):
                a = a_ref[i, pl.ds(variant * 8 * PITCH + w, 8, stride=PITCH), :]
                t = t_ref[i, pl.ds(variant * 8 * PITCH + w, 8, stride=PITCH), :]
                for j in range(STA):
                    c = c_ref[j, pl.ds(w, 8, stride=PITCH), :]
                    v = a * c
                    p[j] = v if w == 0 else p[j] + v
                    v = t * c
                    q[j] = v if w == 0 else q[j] + v
            values = [joined(p[j], q[j]) for j in range(STA)] + [zero]
            for j in range(0, 8, 2):
                pair = jnp.concatenate([values[j], values[j + 1]], axis=0).astype(BF16)
                x_ref[i, (variant * 8 + j) * 8:(variant * 8 + j + 2) * 8, :] = pair
        return carry

    lax.fori_loop(0, STA, per_station, 0)
    total = part_ref[...]
    for i in range(STA):
        total = total + jnp.dot(hot_ref[:, i * LANES:(i + 1) * LANES], x_ref[i], preferred_element_type=F32)
    for w, tile in enumerate(chunk_transpose([total[k * 64:(k + 1) * 64, :] for k in range(CAP)])):
        out_ref[pl.ds(w, 64, stride=4), :] = tile


def finish_kernel(in_ref, out_ref, s_ref):
    total = in_ref[0]
    for z in range(1, 8):
        total = total + in_ref[z]
    s_ref[...] = total * (1.0 / 64.0)
    tiles = chunk_transpose([s_ref[pl.ds(m, 8, stride=4), :] for m in range(4)])
    for k in range(CAP):
        for t in range(8):
            out_ref[k:k + 1, t * LANES:(t + 1) * LANES] = tiles[k][t:t + 1, :]


def on_device(spectra, pair_bins, owner_count, bin_order):
    vmem = pl.BlockSpec(memory_space=pltpu.VMEM)
    packed = pl.pallas_call(
        pack_kernel,
        out_shape=pltpu.VMEM((32, MSG, LANES), BF16),
        in_specs=[pl.BlockSpec(memory_space=pl.ANY), vmem],
        out_specs=vmem,
        scratch_shapes=[pltpu.VMEM((STA, WIN, 4096), BF16), pltpu.SemaphoreType.DMA((STA,))],
        name="pack",
    )(jnp.transpose(spectra, (1, 0, 2)), jnp.transpose(pair_bins, (1, 0, 2)))
    own = lax.all_to_all(packed, ("y", "c", "win"), 0, 0)
    count = lax.axis_size("z")
    halo = lax.ppermute(own[24:32], "z", [(i, (i + 1) % count) for i in range(count)])
    own = pltpu.with_memory_space_constraint(own, pltpu.VMEM)
    part, edge_hot = pl.pallas_call(
        cross_kernel,
        out_shape=(pltpu.VMEM((256, LANES), F32), pltpu.VMEM((256, STA * LANES), BF16)),
        in_specs=[vmem] * 3,
        out_specs=(vmem, vmem),
        scratch_shapes=[
            pltpu.VMEM((STA, 176, LANES), F32),
            pltpu.VMEM((STA, 144, LANES), F32),
            pltpu.VMEM((STA, 64, LANES), F32),
            pltpu.VMEM((STA * KI, NG * LANES), BF16),
            pltpu.VMEM((256, STA * KI), BF16),
        ],
        name="cross",
    )(own, owner_count.reshape(1, -1), bin_order.reshape(1, -1))
    halo = pltpu.with_memory_space_constraint(halo, pltpu.VMEM)
    send = pl.pallas_call(
        edge_kernel,
        out_shape=pltpu.VMEM((256, LANES), F32),
        in_specs=[vmem] * 4,
        out_specs=vmem,
        scratch_shapes=[
            pltpu.VMEM((STA, 16 * PITCH, LANES), F32),
            pltpu.VMEM((STA, 16 * PITCH, LANES), F32),
            pltpu.VMEM((STA, 8 * PITCH, LANES), F32),
            pltpu.VMEM((STA, LANES, LANES), BF16),
        ],
        name="edge",
    )(own, halo, *(pltpu.with_memory_space_constraint(v, pltpu.VMEM) for v in (part, edge_hot)))
    got = lax.all_to_all(send.reshape(256, 1, LANES), ("z", "y", "c", "win"), 0, 0)
    got = pltpu.with_memory_space_constraint(got.reshape(8, 32, LANES), pltpu.VMEM)
    return pl.pallas_call(
        finish_kernel,
        out_shape=jax.ShapeDtypeStruct((CAP, 1024), F32),
        in_specs=[vmem],
        out_specs=vmem,
        scratch_shapes=[pltpu.VMEM((32, LANES), F32)],
        name="finish",
    )(got)


def solution(mesh):
    fine = Mesh(mesh.devices.reshape(8, 4, 2, 4), ("z", "y", "c", "win"))
    sta = ("z", "y", "c")
    return jax.shard_map(
        on_device,
        mesh=fine,
        in_specs=(P("win", sta, None), P(sta, None, None), P(), P()),
        out_specs=P(sta, "win"),
        check_vma=False,
    )
```

```python
import jax
import jax.numpy as jnp
from jax import lax
from jax.experimental import pallas as pl
from jax.experimental.pallas import tpu as pltpu
from jax.sharding import Mesh, PartitionSpec as P

PLANE = 8
STA = 7
WIN = 16
NG = 4
ROUNDS = 3
CAP = 4
ROWS = STA * WIN
MSG = ROWS + 8
PITCH = WIN + 1
LANES = 128
CHUNK = 32
KI = 256
F32 = jnp.float32
BF16 = jnp.bfloat16


def lane_iota(shape):
    return lax.broadcasted_iota(jnp.int32, shape, len(shape) - 1)


def chunk_transpose(tiles):
    lane = lane_iota(tiles[0].shape)
    low = lane < 64
    even = (lane % 64) < CHUNK
    axis = tiles[0].ndim - 1

    def half(a, b):
        return jnp.where(low, a, pltpu.roll(b, 64, axis)), jnp.where(low, pltpu.roll(a, 64, axis), b)

    def quarter(a, b):
        return jnp.where(even, a, pltpu.roll(b, CHUNK, axis)), jnp.where(even, pltpu.roll(a, LANES - CHUNK, axis), b)

    u0, u2 = half(tiles[0], tiles[2])
    u1, u3 = half(tiles[1], tiles[3])
    v0, v1 = quarter(u0, u1)
    v2, v3 = quarter(u2, u3)
    return v0, v1, v2, v3


def pack_kernel(x_hbm, bins_hbm, out_ref, x_ref, bins_ref, sems, bins_sem):
    def station(s):
        return pltpu.make_async_copy(x_hbm.at[s], x_ref.at[s], sems.at[s])

    bins_copy = pltpu.make_async_copy(bins_hbm, bins_ref, bins_sem)
    bins_copy.start()
    for s in range(STA):
        station(s).start()
    bins_copy.wait()
    lane8 = lax.broadcasted_iota(jnp.int32, (STA, LANES), 1)
    row8 = lax.broadcasted_iota(jnp.int32, (STA, LANES), 0)
    labels = jnp.zeros((STA, LANES), F32)
    for r in range(ROUNDS):
        place = jnp.where(lane8 == row8 + 8 * r, 1.0, 0.0).astype(F32)
        labels = labels + jnp.dot(bins_ref[r].astype(F32), place, preferred_element_type=F32)
    labels = jnp.concatenate([labels, jnp.zeros((1, LANES), F32)], axis=0).astype(BF16)
    for d in range(32):
        out_ref[d, ROWS:MSG, :] = labels

    def step(s, carry):
        station(s).wait()
        rows = pl.ds(pl.multiple_of(s * WIN, WIN), WIN)
        for q in range(8):
            tiles = [x_ref[s, :, n * 1024 + q * LANES:n * 1024 + (q + 1) * LANES] for n in range(4)]
            for m, tile in enumerate(chunk_transpose(tiles)):
                out_ref[4 * q + m, rows, :] = tile
        return carry

    lax.fori_loop(0, STA, step, 0)


def slot_bins(count_ref, order_ref):
    row = lax.broadcasted_iota(jnp.int32, (64, 64), 0)
    lane = lax.broadcasted_iota(jnp.int32, (64, 64), 1)
    counts = jnp.broadcast_to(count_ref[...].astype(F32), (64, 64))
    start = jnp.sum(jnp.where(lane < row, counts, 0.0), axis=1, keepdims=True)
    count = jnp.sum(jnp.where(lane == row, counts, 0.0), axis=1, keepdims=True)
    lane = lax.broadcasted_iota(jnp.int32, (64, LANES), 1).astype(F32)
    order = jnp.broadcast_to(order_ref[...].astype(F32), (64, LANES))
    out = []
    for k in range(CAP):
        chosen = jnp.sum(jnp.where(lane == start + float(k), order, 0.0), axis=1, keepdims=True)
        out.append(jnp.where(count > float(k), chosen, -1.0))
    return out


def joined(p, q):
    low = lane_iota(p.shape) < 64
    return jnp.where(low, p, q) + pltpu.roll(jnp.where(low, q, p), 64, 1)


def cross_kernel(own_ref, count_ref, order_ref, out_ref, edge_hot_ref, t_ref, s_ref, m_ref, e_ref, d_ref, f_ref, x_ref, hot_ref):
    lane = lane_iota((8, LANES))
    low = lane < 64
    zero = jnp.zeros((8, LANES), F32)

    spread = jnp.where(lax.broadcasted_iota(jnp.int32, (LANES, KI), 1) // 8
                       == lax.broadcasted_iota(jnp.int32, (LANES, KI), 0), 1.0, 0.0)
    lane_q = lane_iota((8, KI))
    qmod = lane_q % 8
    labels = jnp.zeros((8, KI), F32)
    for b in range(PLANE):
        wide = jnp.dot(own_ref[b * NG, ROWS:MSG, :].astype(F32), spread, preferred_element_type=F32)
        labels = labels + jnp.where(qmod == b, wide, 0.0)
    labels = jnp.where(lane_q // 64 > qmod, -2.0, labels)

    col = lane_iota((LANES, LANES))
    row = lax.broadcasted_iota(jnp.int32, (LANES, LANES), 0)
    variant, half, station = col // 64, (col % 8) // 4, (col // 8) % 8
    first = jnp.where((variant == 0) & (row == (1 + half) * 8 + station), 1.0, 0.0).astype(F32)
    second = jnp.where((variant == 1) & (row == 2 * 8 + station), 1.0, 0.0).astype(F32)
    edge = jnp.dot(own_ref[0, ROWS:MSG, :].astype(F32), first, preferred_element_type=F32)
    edge = edge + jnp.dot(own_ref[NG, ROWS:MSG, :].astype(F32), second, preferred_element_type=F32)
    lane_e = lane_iota((8, LANES))
    edge = jnp.where((lane_e >= 64) & (lane_e % 8 >= 4), -2.0, edge)

    bins = [jnp.broadcast_to(v, (64, KI)) for v in slot_bins(count_ref, order_ref)]
    for i in range(STA):
        row = jnp.broadcast_to(labels[i:i + 1, :], (64, KI))
        edge_row = jnp.broadcast_to(edge[i:i + 1, :], (64, LANES))
        for k in range(CAP):
            rows = slice(k * 64, (k + 1) * 64)
            hot_ref[rows, i * KI:(i + 1) * KI] = jnp.where(bins[k] == row, 1.0, 0.0).astype(BF16)
            edge_hot_ref[rows, i * LANES:(i + 1) * LANES] = jnp.where(
                bins[k][:, :LANES] == edge_row, 1.0, 0.0).astype(BF16)

    for i in range(STA):
        f_ref[i, STA * 8:(STA + 1) * 8, :] = zero
        x_ref[i * KI + ROUNDS * 64:(i + 1) * KI, :] = jnp.zeros((64, NG * LANES), BF16)
        m_ref[i, 0:2 * PITCH, :] = jnp.zeros((2 * PITCH, LANES), F32)

    def per_shard(g, carry):
        low_rows = lane_iota((ROWS, LANES)) < 64
        before = [jnp.zeros((ROWS, LANES), F32)] * 2
        turned_before = jnp.zeros((ROWS, LANES), F32)
        for b in range(PLANE):
            piece = own_ref[b * NG + g, 0:ROWS, :].astype(F32)
            turned = pltpu.roll(piece, 64, 1)
            total = piece + turned
            mixed = jnp.where(low_rows, piece - turned, total)
            shared = jnp.where(low_rows, before[0], before[1])
            for s in range(STA):
                rows = slice(s * WIN, (s + 1) * WIN)
                own_rows = slice(b * PITCH, b * PITCH + WIN)
                t_ref[s, own_rows, :] = turned[rows]
                s_ref[s, own_rows, :] = total[rows]
                m_ref[s, (b + 2) * PITCH:(b + 2) * PITCH + WIN, :] = mixed[rows]
                e_ref[s, own_rows, :] = shared[rows]
                if s % 2 == 1:
                    d_ref[s // 2, own_rows, :] = jnp.where(
                        low_rows[:WIN], piece[rows], turned[(s + 1) * WIN:(s + 2) * WIN])
            before = [piece, turned_before]
            turned_before = turned

        lanes = pl.ds(pl.multiple_of(g * LANES, LANES), LANES)

        def add(acc, key, w, v):
            acc[key] = v if w == 0 else acc[key] + v

        def spread_of(k):
            turned = pltpu.roll(k, 64, 1)
            return jnp.where(low, k, turned), jnp.where(low, turned, k)

        for i in range(STA):
            k1, k1_own, k23 = {}, {}, {}
            pairs = [n for n in range(3) if 2 * n + 2 > i]
            for w in range(WIN):
                rows = pl.ds(w, 8, stride=PITCH)
                t = t_ref[i, rows, :]
                total = s_ref[i, rows, :]
                add(k23, (0, i), w, t * t)
                for j in range(i + 1, STA):
                    add(k23, (0, j), w, t * m_ref[j, pl.ds(2 * PITCH + w, 8, stride=PITCH), :])
                for n in pairs:
                    add(k1_own, n, w, total * d_ref[n, rows, :])
            auto = k23[0, i]
            f_ref[i, i * 8:(i + 1) * 8, :] = jnp.where(low, auto + pltpu.roll(auto, 64, 1), 0.0)
            for n in pairs:
                for j, k in zip((2 * n + 1, 2 * n + 2), spread_of(k1_own[n])):
                    if j > i:
                        value = k - k23[0, j]
                        f_ref[i, j * 8:(j + 1) * 8, :] = value
                        f_ref[j, i * 8:(i + 1) * 8, :] = jnp.where(low, value, -value)
            for w in range(WIN):
                rows = pl.ds(w, 8, stride=PITCH)
                t = t_ref[i, rows, :]
                total = s_ref[i, rows, :]
                for j in range(STA):
                    add(k23, (1, j), w, t * m_ref[j, pl.ds(PITCH + w, 8, stride=PITCH), :])
                    add(k23, (2, j), w, t * m_ref[j, rows, :])
                    add(k1, j, w, total * e_ref[j, rows, :])
            values = {(1, STA): zero, (2, STA): zero}
            for j in range(STA):
                for r, k in zip((1, 2), spread_of(k1[j])):
                    values[r, j] = k - k23[r, j]
            for r in (1, 2):
                for j in range(0, 8, 2):
                    pair = jnp.concatenate([values[r, j], values[r, j + 1]], axis=0).astype(BF16)
                    base = i * KI + (r * 8 + j) * 8
                    x_ref[base:base + 16, lanes] = pair
        for i in range(STA):
            x_ref[i * KI:i * KI + 64, lanes] = f_ref[i].astype(BF16)
        return carry

    lax.fori_loop(0, NG, per_shard, 0)
    total = jnp.dot(hot_ref[...], x_ref[...], preferred_element_type=F32)
    out_ref[...] = (total[:, 0:128] + total[:, 128:256]) + (total[:, 256:384] + total[:, 384:512])


def edge_kernel(own_ref, halo_ref, part_ref, hot_ref, out_ref, a_ref, t_ref, c_ref, x_ref):
    sign = jnp.where(lane_iota((ROWS, LANES)) < 64, 1.0, -1.0).astype(F32)
    zero = jnp.zeros((8, LANES), F32)
    for g in range(NG):
        for slot, (ref, index) in enumerate(((own_ref, g), (own_ref, NG + g), (halo_ref, NG + g), (halo_ref, g))):
            piece = ref[index, 0:ROWS, :].astype(F32)
            for s in range(STA):
                rows = piece[s * WIN:(s + 1) * WIN]
                if slot >= 2:
                    base = ((slot - 2) * 4 + g) * PITCH
                    c_ref[s, base:base + WIN, :] = rows
                else:
                    for half in range(2):
                        base = (slot * 8 + half * 4 + g) * PITCH
                        a_ref[s, base:base + WIN, :] = rows
            if slot < 2:
                turned = pltpu.roll(piece, 64, 1) * sign
                for s in range(STA):
                    for half in range(2):
                        base = (slot * 8 + half * 4 + g) * PITCH
                        t_ref[s, base:base + WIN, :] = turned[s * WIN:(s + 1) * WIN]

    def per_station(i, carry):
        for variant in range(2):
            p, q = {}, {}
            for w in range(WIN):
                a = a_ref[i, pl.ds(variant * 8 * PITCH + w, 8, stride=PITCH), :]
                t = t_ref[i, pl.ds(variant * 8 * PITCH + w, 8, stride=PITCH), :]
                for j in range(STA):
                    c = c_ref[j, pl.ds(w, 8, stride=PITCH), :]
                    v = a * c
                    p[j] = v if w == 0 else p[j] + v
                    v = t * c
                    q[j] = v if w == 0 else q[j] + v
            values = [joined(p[j], q[j]) for j in range(STA)] + [zero]
            for j in range(0, 8, 2):
                pair = jnp.concatenate([values[j], values[j + 1]], axis=0).astype(BF16)
                x_ref[i, (variant * 8 + j) * 8:(variant * 8 + j + 2) * 8, :] = pair
        return carry

    lax.fori_loop(0, STA, per_station, 0)
    total = part_ref[...]
    for i in range(STA):
        total = total + jnp.dot(hot_ref[:, i * LANES:(i + 1) * LANES], x_ref[i], preferred_element_type=F32)
    for w, tile in enumerate(chunk_transpose([total[k * 64:(k + 1) * 64, :] for k in range(CAP)])):
        out_ref[pl.ds(w, 64, stride=4), :] = tile


def finish_kernel(in_ref, out_ref, s_ref):
    total = in_ref[0]
    for z in range(1, 8):
        total = total + in_ref[z]
    s_ref[...] = total * (1.0 / 64.0)
    tiles = chunk_transpose([s_ref[pl.ds(m, 8, stride=4), :] for m in range(4)])
    for k in range(CAP):
        for t in range(8):
            out_ref[k:k + 1, t * LANES:(t + 1) * LANES] = tiles[k][t:t + 1, :]


def in_vmem(value):
    return pltpu.with_memory_space_constraint(value, pltpu.VMEM)


def on_device(spectra, pair_bins, owner_count, bin_order):
    vmem = pl.BlockSpec(memory_space=pltpu.VMEM)
    packed = pl.pallas_call(
        pack_kernel,
        out_shape=pltpu.VMEM((32, MSG, LANES), BF16),
        in_specs=[pl.BlockSpec(memory_space=pl.ANY)] * 2,
        out_specs=vmem,
        scratch_shapes=[
            pltpu.VMEM((STA, WIN, 4096), BF16),
            pltpu.VMEM((ROUNDS, STA, STA), jnp.int32),
            pltpu.SemaphoreType.DMA((STA,)),
            pltpu.SemaphoreType.DMA,
        ],
        name="pack",
    )(jnp.transpose(spectra, (1, 0, 2)), jnp.transpose(pair_bins, (1, 0, 2)))
    own = lax.all_to_all(packed, ("y", "c", "win"), 0, 0)
    count = lax.axis_size("z")
    halo = lax.ppermute(own[24:32], "z", [(i, (i + 1) % count) for i in range(count)])
    own = in_vmem(own)
    part, edge_hot = pl.pallas_call(
        cross_kernel,
        out_shape=(pltpu.VMEM((256, LANES), F32), pltpu.VMEM((256, STA * LANES), BF16)),
        in_specs=[vmem] * 3,
        out_specs=(vmem, vmem),
        scratch_shapes=[
            pltpu.VMEM((STA, 144, LANES), F32),
            pltpu.VMEM((STA, 144, LANES), F32),
            pltpu.VMEM((STA, 176, LANES), F32),
            pltpu.VMEM((STA, 144, LANES), F32),
            pltpu.VMEM((3, 144, LANES), F32),
            pltpu.VMEM((STA, 64, LANES), F32),
            pltpu.VMEM((STA * KI, NG * LANES), BF16),
            pltpu.VMEM((256, STA * KI), BF16),
        ],
        name="cross",
    )(own, in_vmem(owner_count.reshape(1, -1)), in_vmem(bin_order.reshape(1, -1)))
    halo = in_vmem(halo)
    send = pl.pallas_call(
        edge_kernel,
        out_shape=pltpu.VMEM((256, LANES), F32),
        in_specs=[vmem] * 4,
        out_specs=vmem,
        scratch_shapes=[
            pltpu.VMEM((STA, 16 * PITCH, LANES), F32),
            pltpu.VMEM((STA, 16 * PITCH, LANES), F32),
            pltpu.VMEM((STA, 8 * PITCH, LANES), F32),
            pltpu.VMEM((STA, LANES, LANES), BF16),
        ],
        name="edge",
    )(own, halo, in_vmem(part), in_vmem(edge_hot))
    got = lax.all_to_all(send.reshape(256, 1, LANES), ("z", "y", "c", "win"), 0, 0)
    got = in_vmem(got.reshape(8, 32, LANES))
    return pl.pallas_call(
        finish_kernel,
        out_shape=jax.ShapeDtypeStruct((CAP, 1024), F32),
        in_specs=[vmem],
        out_specs=vmem,
        scratch_shapes=[pltpu.VMEM((32, LANES), F32)],
        name="finish",
    )(got)


def solution(mesh):
    fine = Mesh(mesh.devices.reshape(8, 4, 2, 4), ("z", "y", "c", "win"))
    sta = ("z", "y", "c")
    return jax.shard_map(
        on_device,
        mesh=fine,
        in_specs=(P("win", sta, None), P(sta, None, None), P(), P()),
        out_specs=P(sta, "win"),
        check_vma=False,
    )
```

```python
import jax
import jax.numpy as jnp
from jax import lax
from jax.experimental import pallas as pl
from jax.experimental.pallas import tpu as pltpu
from jax.sharding import Mesh, PartitionSpec as P

PLANE = 8
STA = 7
WIN = 16
NG = 4
ROUNDS = 3
CAP = 4
ROWS = STA * WIN
MSG = ROWS + 8
PITCH = WIN + 1
LANES = 128
CHUNK = 32
KI = 256
SMALL = pltpu.CompilerParams(vmem_limit_bytes=16 << 20)
F32 = jnp.float32
BF16 = jnp.bfloat16


def lane_iota(shape):
    return lax.broadcasted_iota(jnp.int32, shape, len(shape) - 1)


def chunk_transpose(tiles):
    lane = lane_iota(tiles[0].shape)
    low = lane < 64
    even = (lane % 64) < CHUNK
    axis = tiles[0].ndim - 1

    def half(a, b):
        return jnp.where(low, a, pltpu.roll(b, 64, axis)), jnp.where(low, pltpu.roll(a, 64, axis), b)

    def quarter(a, b):
        return jnp.where(even, a, pltpu.roll(b, CHUNK, axis)), jnp.where(even, pltpu.roll(a, LANES - CHUNK, axis), b)

    u0, u2 = half(tiles[0], tiles[2])
    u1, u3 = half(tiles[1], tiles[3])
    v0, v1 = quarter(u0, u1)
    v2, v3 = quarter(u2, u3)
    return v0, v1, v2, v3


def pack_kernel(x_hbm, bins_hbm, count_hbm, order_hbm, out_ref, count_ref, order_ref, x_ref, bins_ref, sems, small_sems):
    def station(s):
        return pltpu.make_async_copy(x_hbm.at[s], x_ref.at[s], sems.at[s])

    bins_copy = pltpu.make_async_copy(bins_hbm, bins_ref, small_sems.at[0])
    count_copy = pltpu.make_async_copy(count_hbm, count_ref, small_sems.at[1])
    order_copy = pltpu.make_async_copy(order_hbm, order_ref, small_sems.at[2])
    bins_copy.start()
    for s in range(STA):
        station(s).start()
    count_copy.start()
    order_copy.start()
    bins_copy.wait()
    lane8 = lax.broadcasted_iota(jnp.int32, (STA, LANES), 1)
    row8 = lax.broadcasted_iota(jnp.int32, (STA, LANES), 0)
    labels = jnp.zeros((STA, LANES), F32)
    for r in range(ROUNDS):
        place = jnp.where(lane8 == row8 + 8 * r, 1.0, 0.0).astype(F32)
        labels = labels + jnp.dot(bins_ref[r].astype(F32), place, preferred_element_type=F32)
    labels = jnp.concatenate([labels, jnp.zeros((1, LANES), F32)], axis=0).astype(BF16)
    for d in range(32):
        out_ref[d, ROWS:MSG, :] = labels

    def step(s, carry):
        station(s).wait()
        rows = pl.ds(pl.multiple_of(s * WIN, WIN), WIN)
        for q in range(8):
            tiles = [x_ref[s, :, n * 1024 + q * LANES:n * 1024 + (q + 1) * LANES] for n in range(4)]
            for m, tile in enumerate(chunk_transpose(tiles)):
                out_ref[4 * q + m, rows, :] = tile
        return carry

    lax.fori_loop(0, STA, step, 0)
    count_copy.wait()
    order_copy.wait()


def slot_bins(count_ref, order_ref):
    row = lax.broadcasted_iota(jnp.int32, (64, 64), 0)
    lane = lax.broadcasted_iota(jnp.int32, (64, 64), 1)
    counts = jnp.broadcast_to(count_ref[...].astype(F32), (64, 64))
    start = jnp.sum(jnp.where(lane < row, counts, 0.0), axis=1, keepdims=True)
    count = jnp.sum(jnp.where(lane == row, counts, 0.0), axis=1, keepdims=True)
    lane = lax.broadcasted_iota(jnp.int32, (64, LANES), 1).astype(F32)
    order = jnp.broadcast_to(order_ref[...].astype(F32), (64, LANES))
    out = []
    for k in range(CAP):
        chosen = jnp.sum(jnp.where(lane == start + float(k), order, 0.0), axis=1, keepdims=True)
        out.append(jnp.where(count > float(k), chosen, -1.0))
    return out


def joined(p, q):
    low = lane_iota(p.shape) < 64
    return jnp.where(low, p, q) + pltpu.roll(jnp.where(low, q, p), 64, 1)


def spread_of(k):
    low = lane_iota(k.shape) < 64
    turned = pltpu.roll(k, 64, 1)
    return jnp.where(low, k, turned), jnp.where(low, turned, k)


def cross_kernel(own_ref, count_ref, order_ref, out_ref, edge_hot_ref, edge_t_ref, edge_s_ref,
                 t_ref, s_ref, m_ref, e_ref, d_ref, f_ref, x_ref, hot_ref):
    lane = lane_iota((8, LANES))
    low = lane < 64
    zero = jnp.zeros((8, LANES), F32)

    spread = jnp.where(lax.broadcasted_iota(jnp.int32, (LANES, KI), 1) // 8
                       == lax.broadcasted_iota(jnp.int32, (LANES, KI), 0), 1.0, 0.0).astype(BF16)
    lane_q = lane_iota((8, KI))
    qmod = lane_q % 8
    labels = jnp.zeros((8, KI), F32)
    for b in range(PLANE):
        wide = jnp.dot(own_ref[b * NG, ROWS:MSG, :], spread, preferred_element_type=F32)
        labels = labels + jnp.where(qmod == b, wide, 0.0)
    labels = jnp.where(lane_q // 64 > qmod, -2.0, labels)
    rows_of = [labels[i:i + 1, h * LANES:(h + 1) * LANES] for i in range(STA) for h in range(2)]

    col = lane_iota((LANES, LANES))
    row = lax.broadcasted_iota(jnp.int32, (LANES, LANES), 0)
    half, station = (col % 8) // 4, (col % 64) // 8
    first = jnp.where(row == (1 + half) * 8 + station, 1.0, 0.0).astype(BF16)
    second = jnp.where(row == 2 * 8 + station, 1.0, 0.0).astype(BF16)
    one = jnp.dot(own_ref[0, ROWS:MSG, :], first, preferred_element_type=F32)
    two = jnp.dot(own_ref[NG, ROWS:MSG, :], second, preferred_element_type=F32)
    none = lax.broadcasted_iota(jnp.int32, (8, LANES), 0) == STA
    one = jnp.where(none, -2.0, one)
    two = jnp.where(none, -2.0, two)
    lane_1 = lane_iota((1, LANES))
    upper, second_half = lane_1 >= 64, lane_1 % 8 >= 4
    edge_rows = [jnp.where(upper, one[2 * p + 1:2 * p + 2], one[2 * p:2 * p + 1]) for p in range(4)]
    for p in (0, 2):
        lower_unit = jnp.where(second_half, two[2 * p + 1:2 * p + 2], two[2 * p:2 * p + 1])
        upper_unit = jnp.where(second_half, two[2 * p + 3:2 * p + 4], two[2 * p + 2:2 * p + 3])
        edge_rows.append(jnp.where(upper, upper_unit, lower_unit))

    for k, column in enumerate(slot_bins(count_ref, order_ref)):
        bins = jnp.broadcast_to(column, (64, LANES))
        rows = slice(k * 64, (k + 1) * 64)
        for ref, line in ((hot_ref, rows_of), (edge_hot_ref, edge_rows)):
            for n, wanted in enumerate(line):
                ref[rows, n * LANES:(n + 1) * LANES] = jnp.where(
                    bins == jnp.broadcast_to(wanted, (64, LANES)), 1.0, 0.0).astype(BF16)

    for i in range(STA):
        f_ref[i, STA * 8:(STA + 1) * 8, :] = zero
        x_ref[i * KI + ROUNDS * 64:(i + 1) * KI, :] = jnp.zeros((64, NG * LANES), BF16)
        m_ref[i, 0:2 * PITCH, :] = jnp.zeros((2 * PITCH, LANES), F32)

    def per_shard(g, carry):
        low_rows = lane_iota((ROWS, LANES)) < 64
        before = [jnp.zeros((ROWS, LANES), F32)] * 2
        turned_before = jnp.zeros((ROWS, LANES), F32)
        for b in range(PLANE):
            piece = own_ref[b * NG + g, 0:ROWS, :].astype(F32)
            turned = pltpu.roll(piece, 64, 1)
            total = piece + turned
            mixed = jnp.where(low_rows, piece - turned, total)
            shared = jnp.where(low_rows, before[0], before[1])
            for s in range(STA):
                rows = slice(s * WIN, (s + 1) * WIN)
                own_rows = slice(b * PITCH, b * PITCH + WIN)
                t_ref[s, own_rows, :] = turned[rows]
                s_ref[s, own_rows, :] = total[rows]
                m_ref[s, (b + 2) * PITCH:(b + 2) * PITCH + WIN, :] = mixed[rows]
                e_ref[s, own_rows, :] = shared[rows]
                if s % 2 == 1:
                    d_ref[s // 2, own_rows, :] = jnp.where(
                        low_rows[:WIN], piece[rows], turned[(s + 1) * WIN:(s + 2) * WIN])
            if b < 2:
                for s in range(STA):
                    for half in range(2):
                        if b == 1 and s % 2 != half and s != STA - 1:
                            continue
                        unit = s if b == 0 else STA + s // 2
                        base = (half * NG + g) * PITCH
                        edge_t_ref[unit, pl.ds(base, WIN), :] = turned[s * WIN:(s + 1) * WIN]
                        edge_s_ref[unit, pl.ds(base, WIN), :] = total[s * WIN:(s + 1) * WIN]
            before = [piece, turned_before]
            turned_before = turned

        lanes = pl.ds(pl.multiple_of(g * LANES, LANES), LANES)

        def add(acc, key, w, v):
            acc[key] = v if w == 0 else acc[key] + v

        for i in range(STA):
            k1, k1_own, k23 = {}, {}, {}
            pairs = [n for n in range(3) if 2 * n + 2 > i]
            for w in range(WIN):
                rows = pl.ds(w, 8, stride=PITCH)
                t = t_ref[i, rows, :]
                total = s_ref[i, rows, :]
                add(k23, (0, i), w, t * t)
                for j in range(i + 1, STA):
                    add(k23, (0, j), w, t * m_ref[j, pl.ds(2 * PITCH + w, 8, stride=PITCH), :])
                for n in pairs:
                    add(k1_own, n, w, total * d_ref[n, rows, :])
            auto = k23[0, i]
            f_ref[i, i * 8:(i + 1) * 8, :] = jnp.where(low, auto + pltpu.roll(auto, 64, 1), 0.0)
            for n in pairs:
                for j, k in zip((2 * n + 1, 2 * n + 2), spread_of(k1_own[n])):
                    if j > i:
                        value = k - k23[0, j]
                        f_ref[i, j * 8:(j + 1) * 8, :] = value
                        f_ref[j, i * 8:(i + 1) * 8, :] = jnp.where(low, value, -value)
            for w in range(WIN):
                rows = pl.ds(w, 8, stride=PITCH)
                t = t_ref[i, rows, :]
                total = s_ref[i, rows, :]
                for j in range(STA):
                    add(k23, (1, j), w, t * m_ref[j, pl.ds(PITCH + w, 8, stride=PITCH), :])
                    add(k23, (2, j), w, t * m_ref[j, rows, :])
                    add(k1, j, w, total * e_ref[j, rows, :])
            values = {(1, STA): zero, (2, STA): zero}
            for j in range(STA):
                for r, k in zip((1, 2), spread_of(k1[j])):
                    values[r, j] = k - k23[r, j]
            for r in (1, 2):
                for j in range(0, 8, 2):
                    pair = jnp.concatenate([values[r, j], values[r, j + 1]], axis=0).astype(BF16)
                    base = i * KI + (r * 8 + j) * 8
                    x_ref[base:base + 16, lanes] = pair
        for i in range(STA):
            x_ref[i * KI:i * KI + 64, lanes] = f_ref[i].astype(BF16)
        return carry

    lax.fori_loop(0, NG, per_shard, 0)
    total = jnp.dot(hot_ref[...], x_ref[...], preferred_element_type=F32)
    out_ref[...] = (total[:, 0:128] + total[:, 128:256]) + (total[:, 256:384] + total[:, 384:512])


def edge_kernel(halo_ref, part_ref, hot_ref, t_ref, s_ref, out_ref, m_ref, d_ref, x_ref):
    low = lane_iota((WIN, LANES)) < 64
    low_rows = lane_iota((ROWS, LANES)) < 64
    zero = jnp.zeros((8, LANES), F32)
    for g in range(NG):
        for half in range(2):
            piece = halo_ref[(1 - half) * NG + g, 0:ROWS, :].astype(F32)
            turned = pltpu.roll(piece, 64, 1)
            mixed = jnp.where(low_rows, piece - turned, piece + turned)
            bases = [(0, (half * NG + g) * PITCH)]
            if half == 0:
                bases += [(1, g * PITCH), (1, (NG + g) * PITCH)]
            for s in range(STA):
                for kind, base in bases:
                    m_ref[kind * STA + s, base:base + WIN, :] = mixed[s * WIN:(s + 1) * WIN]
            for n in range(4):
                s, t = 2 * n, min(2 * n + 1, STA - 1)
                shared = jnp.where(low, piece[s * WIN:(s + 1) * WIN], turned[t * WIN:(t + 1) * WIN])
                for kind, base in bases:
                    d_ref[kind * 4 + n, base:base + WIN, :] = shared

    x_ref[3 * LANES + 64:4 * LANES, :] = jnp.zeros((64, LANES), BF16)
    for unit in range(STA + 4):
        kind = 0 if unit < STA else 1
        k1, k23 = {}, {}
        for w in range(WIN):
            rows = pl.ds(w, 8, stride=PITCH)
            t = t_ref[unit, rows, :]
            total = s_ref[unit, rows, :]
            for j in range(STA):
                v = t * m_ref[kind * STA + j, rows, :]
                k23[j] = v if w == 0 else k23[j] + v
            for n in range(4):
                v = total * d_ref[kind * 4 + n, rows, :]
                k1[n] = v if w == 0 else k1[n] + v
        base = (unit if kind == 0 else unit + 1) * 64
        for n in range(4):
            lower, upper = spread_of(k1[n])
            values = [lower - k23[2 * n], upper - k23[2 * n + 1] if n < 3 else zero]
            x_ref[base + n * 16:base + (n + 1) * 16, :] = jnp.concatenate(values, axis=0).astype(BF16)
    total = part_ref[...] + jnp.dot(hot_ref[...], x_ref[...], preferred_element_type=F32)
    for w, tile in enumerate(chunk_transpose([total[k * 64:(k + 1) * 64, :] for k in range(CAP)])):
        out_ref[pl.ds(w, 64, stride=4), :] = tile


def finish_kernel(in_ref, out_ref, s_ref):
    total = in_ref[0]
    for z in range(1, 8):
        total = total + in_ref[z]
    s_ref[...] = total * (1.0 / 64.0)
    tiles = chunk_transpose([s_ref[pl.ds(m, 8, stride=4), :] for m in range(4)])
    for k in range(CAP):
        for t in range(8):
            out_ref[k:k + 1, t * LANES:(t + 1) * LANES] = tiles[k][t:t + 1, :]


def in_vmem(value):
    return pltpu.with_memory_space_constraint(value, pltpu.VMEM)


def on_device(spectra, pair_bins, owner_count, bin_order):
    vmem = pl.BlockSpec(memory_space=pltpu.VMEM)
    in_hbm = pl.BlockSpec(memory_space=pl.ANY)
    packed, counts, order = pl.pallas_call(
        pack_kernel,
        out_shape=(
            pltpu.VMEM((32, MSG, LANES), BF16),
            pltpu.VMEM((1, owner_count.shape[0]), jnp.int32),
            pltpu.VMEM((1, bin_order.shape[0]), jnp.int32),
        ),
        in_specs=[in_hbm] * 4,
        out_specs=(vmem,) * 3,
        scratch_shapes=[
            pltpu.VMEM((STA, WIN, 4096), BF16),
            pltpu.VMEM((ROUNDS, STA, STA), jnp.int32),
            pltpu.SemaphoreType.DMA((STA,)),
            pltpu.SemaphoreType.DMA((3,)),
        ],
        name="pack",
    )(
        jnp.transpose(spectra, (1, 0, 2)),
        jnp.transpose(pair_bins, (1, 0, 2)),
        owner_count.reshape(1, -1),
        bin_order.reshape(1, -1),
    )
    own = lax.all_to_all(packed, ("y", "c", "win"), 0, 0)
    count = lax.axis_size("z")
    halo = lax.ppermute(own[24:32], "z", [(i, (i + 1) % count) for i in range(count)])
    units = STA + 4
    between = pl.pallas_call(
        cross_kernel,
        out_shape=(
            pltpu.VMEM((256, LANES), F32),
            pltpu.VMEM((256, 6 * LANES), BF16),
            pltpu.VMEM((units, 8 * PITCH, LANES), F32),
            pltpu.VMEM((units, 8 * PITCH, LANES), F32),
        ),
        in_specs=[vmem] * 3,
        out_specs=(vmem,) * 4,
        scratch_shapes=[
            pltpu.VMEM((STA, 144, LANES), F32),
            pltpu.VMEM((STA, 144, LANES), F32),
            pltpu.VMEM((STA, 176, LANES), F32),
            pltpu.VMEM((STA, 144, LANES), F32),
            pltpu.VMEM((3, 144, LANES), F32),
            pltpu.VMEM((STA, 64, LANES), F32),
            pltpu.VMEM((STA * KI, NG * LANES), BF16),
            pltpu.VMEM((256, STA * KI), BF16),
        ],
        compiler_params=SMALL,
        name="cross",
    )(in_vmem(own), in_vmem(counts), in_vmem(order))
    send = pl.pallas_call(
        edge_kernel,
        out_shape=pltpu.VMEM((256, LANES), F32),
        in_specs=[vmem] * 5,
        out_specs=vmem,
        scratch_shapes=[
            pltpu.VMEM((2 * STA, 8 * PITCH, LANES), F32),
            pltpu.VMEM((8, 8 * PITCH, LANES), F32),
            pltpu.VMEM((6 * LANES, LANES), BF16),
        ],
        compiler_params=SMALL,
        name="edge",
    )(in_vmem(halo), *(in_vmem(v) for v in between))
    got = lax.all_to_all(send.reshape(256, 1, LANES), ("z", "y", "c", "win"), 0, 0)
    got = in_vmem(got.reshape(8, 32, LANES))
    return pl.pallas_call(
        finish_kernel,
        out_shape=jax.ShapeDtypeStruct((CAP, 1024), F32),
        in_specs=[vmem],
        out_specs=vmem,
        scratch_shapes=[pltpu.VMEM((32, LANES), F32)],
        compiler_params=SMALL,
        name="finish",
    )(got)


def solution(mesh):
    fine = Mesh(mesh.devices.reshape(8, 4, 2, 4), ("z", "y", "c", "win"))
    sta = ("z", "y", "c")
    return jax.shard_map(
        on_device,
        mesh=fine,
        in_specs=(P("win", sta, None), P(sta, None, None), P(), P()),
        out_specs=P(sta, "win"),
        check_vma=False,
    )
```

```python
import jax
import jax.numpy as jnp
from jax import lax
from jax.experimental import pallas as pl
from jax.experimental.pallas import tpu as pltpu
from jax.sharding import Mesh, PartitionSpec as P

PLANE = 8
STA = 7
WIN = 16
NG = 4
ROUNDS = 3
CAP = 4
ROWS = STA * WIN
MSG = ROWS + 8
PITCH = WIN + 1
LANES = 128
CHUNK = 32
KI = 256
SMALL = pltpu.CompilerParams(vmem_limit_bytes=16 << 20)
F32 = jnp.float32
BF16 = jnp.bfloat16


def lane_iota(shape):
    return lax.broadcasted_iota(jnp.int32, shape, len(shape) - 1)


def chunk_transpose(tiles):
    lane = lane_iota(tiles[0].shape)
    low = lane < 64
    even = (lane % 64) < CHUNK
    axis = tiles[0].ndim - 1

    def diagonals(a, b, c, d):
        ab, cd = jnp.where(even, a, b), jnp.where(even, c, d)
        bc, da = jnp.where(even, b, c), jnp.where(even, d, a)
        return jnp.where(low, ab, cd), jnp.where(low, bc, da), jnp.where(low, cd, ab), jnp.where(low, da, bc)

    g0, g1, g2, g3 = diagonals(*tiles)
    v0, v3, v2, v1 = diagonals(g0, *(pltpu.roll(g, k * CHUNK, axis) for k, g in ((1, g1), (2, g2), (3, g3))))
    return v0, v1, v2, v3


def pack_kernel(x_hbm, bins_hbm, count_hbm, order_hbm, out_ref, count_ref, order_ref, x_ref, bins_ref, sems, small_sems):
    def station(s):
        return pltpu.make_async_copy(x_hbm.at[s], x_ref.at[s], sems.at[s])

    bins_copy = pltpu.make_async_copy(bins_hbm, bins_ref, small_sems.at[0])
    count_copy = pltpu.make_async_copy(count_hbm, count_ref, small_sems.at[1])
    order_copy = pltpu.make_async_copy(order_hbm, order_ref, small_sems.at[2])
    bins_copy.start()
    for s in range(STA):
        station(s).start()
    count_copy.start()
    order_copy.start()
    bins_copy.wait()
    lane8 = lax.broadcasted_iota(jnp.int32, (STA, LANES), 1)
    row8 = lax.broadcasted_iota(jnp.int32, (STA, LANES), 0)
    labels = jnp.zeros((STA, LANES), F32)
    for r in range(ROUNDS):
        place = jnp.where(lane8 == row8 + 8 * r, 1.0, 0.0).astype(F32)
        labels = labels + jnp.dot(bins_ref[r].astype(F32), place, preferred_element_type=F32)
    labels = jnp.concatenate([labels, jnp.zeros((1, LANES), F32)], axis=0).astype(BF16)
    for d in range(32):
        out_ref[d, ROWS:MSG, :] = labels

    def step(s, carry):
        station(s).wait()
        rows = pl.ds(pl.multiple_of(s * WIN, WIN), WIN)
        for q in range(8):
            tiles = [x_ref[s, :, n * 1024 + q * LANES:n * 1024 + (q + 1) * LANES] for n in range(4)]
            for m, tile in enumerate(chunk_transpose(tiles)):
                out_ref[4 * q + m, rows, :] = tile
        return carry

    lax.fori_loop(0, STA, step, 0)
    count_copy.wait()
    order_copy.wait()


def slot_bins(count_ref, order_ref):
    row = lax.broadcasted_iota(jnp.int32, (64, 64), 0)
    lane = lax.broadcasted_iota(jnp.int32, (64, 64), 1)
    counts = jnp.broadcast_to(count_ref[...].astype(F32), (64, 64))
    start = jnp.sum(jnp.where(lane < row, counts, 0.0), axis=1, keepdims=True)
    count = jnp.sum(jnp.where(lane == row, counts, 0.0), axis=1, keepdims=True)
    lane = lax.broadcasted_iota(jnp.int32, (64, LANES), 1).astype(F32)
    order = jnp.broadcast_to(order_ref[...].astype(F32), (64, LANES))
    out = []
    for k in range(CAP):
        chosen = jnp.sum(jnp.where(lane == start + float(k), order, 0.0), axis=1, keepdims=True)
        out.append(jnp.where(count > float(k), chosen, -1.0))
    return out


def joined(p, q):
    low = lane_iota(p.shape) < 64
    return jnp.where(low, p, q) + pltpu.roll(jnp.where(low, q, p), 64, 1)


def spread_of(k):
    low = lane_iota(k.shape) < 64
    turned = pltpu.roll(k, 64, 1)
    return jnp.where(low, k, turned), jnp.where(low, turned, k)


def cross_kernel(own_ref, count_ref, order_ref, out_ref, edge_hot_ref, edge_t_ref, edge_s_ref,
                 t_ref, s_ref, m_ref, e_ref, d_ref, f_ref, x_ref, hot_ref):
    lane = lane_iota((8, LANES))
    low = lane < 64
    zero = jnp.zeros((8, LANES), F32)

    spread = jnp.where(lax.broadcasted_iota(jnp.int32, (LANES, KI), 1) // 8
                       == lax.broadcasted_iota(jnp.int32, (LANES, KI), 0), 1.0, 0.0).astype(BF16)
    lane_q = lane_iota((8, KI))
    qmod = lane_q % 8
    labels = jnp.zeros((8, KI), F32)
    for b in range(PLANE):
        wide = jnp.dot(own_ref[b * NG, ROWS:MSG, :], spread, preferred_element_type=F32)
        labels = labels + jnp.where(qmod == b, wide, 0.0)
    labels = jnp.where(lane_q // 64 > qmod, -2.0, labels)
    rows_of = [labels[i:i + 1, h * LANES:(h + 1) * LANES] for i in range(STA) for h in range(2)]

    col = lane_iota((LANES, LANES))
    row = lax.broadcasted_iota(jnp.int32, (LANES, LANES), 0)
    half, station = (col % 8) // 4, (col % 64) // 8
    first = jnp.where(row == (1 + half) * 8 + station, 1.0, 0.0).astype(BF16)
    second = jnp.where(row == 2 * 8 + station, 1.0, 0.0).astype(BF16)
    one = jnp.dot(own_ref[0, ROWS:MSG, :], first, preferred_element_type=F32)
    two = jnp.dot(own_ref[NG, ROWS:MSG, :], second, preferred_element_type=F32)
    none = lax.broadcasted_iota(jnp.int32, (8, LANES), 0) == STA
    one = jnp.where(none, -2.0, one)
    two = jnp.where(none, -2.0, two)
    lane_1 = lane_iota((1, LANES))
    upper, second_half = lane_1 >= 64, lane_1 % 8 >= 4
    edge_rows = [jnp.where(upper, one[2 * p + 1:2 * p + 2], one[2 * p:2 * p + 1]) for p in range(4)]
    for p in (0, 2):
        lower_unit = jnp.where(second_half, two[2 * p + 1:2 * p + 2], two[2 * p:2 * p + 1])
        upper_unit = jnp.where(second_half, two[2 * p + 3:2 * p + 4], two[2 * p + 2:2 * p + 3])
        edge_rows.append(jnp.where(upper, upper_unit, lower_unit))

    for k, column in enumerate(slot_bins(count_ref, order_ref)):
        bins = jnp.broadcast_to(column, (64, LANES))
        rows = slice(k * 64, (k + 1) * 64)
        for ref, line in ((hot_ref, rows_of), (edge_hot_ref, edge_rows)):
            for n, wanted in enumerate(line):
                ref[rows, n * LANES:(n + 1) * LANES] = jnp.where(
                    bins == jnp.broadcast_to(wanted, (64, LANES)), 1.0, 0.0).astype(BF16)

    for i in range(STA):
        f_ref[i, STA * 8:(STA + 1) * 8, :] = zero
        x_ref[i * KI + ROUNDS * 64:(i + 1) * KI, :] = jnp.zeros((64, NG * LANES), BF16)
        m_ref[i, 0:2 * PITCH, :] = jnp.zeros((2 * PITCH, LANES), F32)

    def per_shard(g, carry):
        low_rows = lane_iota((ROWS, LANES)) < 64
        before = [jnp.zeros((ROWS, LANES), F32)] * 2
        turned_before = jnp.zeros((ROWS, LANES), F32)
        for b in range(PLANE):
            piece = own_ref[b * NG + g, 0:ROWS, :].astype(F32)
            turned = pltpu.roll(piece, 64, 1)
            total = piece + turned
            mixed = jnp.where(low_rows, piece - turned, total)
            shared = jnp.where(low_rows, before[0], before[1])
            for s in range(STA):
                rows = slice(s * WIN, (s + 1) * WIN)
                own_rows = slice(b * PITCH, b * PITCH + WIN)
                t_ref[s, own_rows, :] = turned[rows]
                s_ref[s, own_rows, :] = total[rows]
                m_ref[s, (b + 2) * PITCH:(b + 2) * PITCH + WIN, :] = mixed[rows]
                e_ref[s, own_rows, :] = shared[rows]
                if s % 2 == 1:
                    d_ref[s // 2, own_rows, :] = jnp.where(
                        low_rows[:WIN], piece[rows], turned[(s + 1) * WIN:(s + 2) * WIN])
            if b < 2:
                for s in range(STA):
                    for half in range(2):
                        if b == 1 and s % 2 != half and s != STA - 1:
                            continue
                        unit = s if b == 0 else STA + s // 2
                        base = (half * NG + g) * PITCH
                        edge_t_ref[unit, pl.ds(base, WIN), :] = turned[s * WIN:(s + 1) * WIN]
                        edge_s_ref[unit, pl.ds(base, WIN), :] = total[s * WIN:(s + 1) * WIN]
            before = [piece, turned_before]
            turned_before = turned

        lanes = pl.ds(pl.multiple_of(g * LANES, LANES), LANES)

        def add(acc, key, w, v):
            acc[key] = v if w == 0 else acc[key] + v

        for i in range(STA):
            k1, k1_own, k23 = {}, {}, {}
            pairs = [n for n in range(3) if 2 * n + 2 > i]
            for w in range(WIN):
                rows = pl.ds(w, 8, stride=PITCH)
                t = t_ref[i, rows, :]
                total = s_ref[i, rows, :]
                add(k23, (0, i), w, t * t)
                for j in range(i + 1, STA):
                    add(k23, (0, j), w, t * m_ref[j, pl.ds(2 * PITCH + w, 8, stride=PITCH), :])
                for n in pairs:
                    add(k1_own, n, w, total * d_ref[n, rows, :])
            auto = k23[0, i]
            f_ref[i, i * 8:(i + 1) * 8, :] = jnp.where(low, auto + pltpu.roll(auto, 64, 1), 0.0)
            for n in pairs:
                for j, k in zip((2 * n + 1, 2 * n + 2), spread_of(k1_own[n])):
                    if j > i:
                        value = k - k23[0, j]
                        f_ref[i, j * 8:(j + 1) * 8, :] = value
                        f_ref[j, i * 8:(i + 1) * 8, :] = jnp.where(low, value, -value)
            for w in range(WIN):
                rows = pl.ds(w, 8, stride=PITCH)
                t = t_ref[i, rows, :]
                total = s_ref[i, rows, :]
                for j in range(STA):
                    add(k23, (1, j), w, t * m_ref[j, pl.ds(PITCH + w, 8, stride=PITCH), :])
                    add(k23, (2, j), w, t * m_ref[j, rows, :])
                    add(k1, j, w, total * e_ref[j, rows, :])
            values = {(1, STA): zero, (2, STA): zero}
            for j in range(STA):
                for r, k in zip((1, 2), spread_of(k1[j])):
                    values[r, j] = k - k23[r, j]
            for r in (1, 2):
                for j in range(0, 8, 2):
                    pair = jnp.concatenate([values[r, j], values[r, j + 1]], axis=0).astype(BF16)
                    base = i * KI + (r * 8 + j) * 8
                    x_ref[base:base + 16, lanes] = pair
        for i in range(STA):
            x_ref[i * KI:i * KI + 64, lanes] = f_ref[i].astype(BF16)
        return carry

    lax.fori_loop(0, NG, per_shard, 0)
    total = jnp.dot(hot_ref[...], x_ref[...], preferred_element_type=F32)
    out_ref[...] = (total[:, 0:128] + total[:, 128:256]) + (total[:, 256:384] + total[:, 384:512])


def edge_kernel(halo_ref, part_ref, hot_ref, t_ref, s_ref, out_ref, m_ref, d_ref, x_ref):
    low = lane_iota((WIN, LANES)) < 64
    low_rows = lane_iota((ROWS, LANES)) < 64
    zero = jnp.zeros((8, LANES), F32)
    for g in range(NG):
        for half in range(2):
            piece = halo_ref[(1 - half) * NG + g, 0:ROWS, :].astype(F32)
            turned = pltpu.roll(piece, 64, 1)
            mixed = jnp.where(low_rows, piece - turned, piece + turned)
            bases = [(0, (half * NG + g) * PITCH)]
            if half == 0:
                bases += [(1, g * PITCH), (1, (NG + g) * PITCH)]
            for s in range(STA):
                for kind, base in bases:
                    m_ref[kind * STA + s, base:base + WIN, :] = mixed[s * WIN:(s + 1) * WIN]
            for n in range(4):
                s, t = 2 * n, min(2 * n + 1, STA - 1)
                shared = jnp.where(low, piece[s * WIN:(s + 1) * WIN], turned[t * WIN:(t + 1) * WIN])
                for kind, base in bases:
                    d_ref[kind * 4 + n, base:base + WIN, :] = shared

    x_ref[3 * LANES + 64:4 * LANES, :] = jnp.zeros((64, LANES), BF16)
    for unit in range(STA + 4):
        kind = 0 if unit < STA else 1
        k1, k23 = {}, {}
        for w in range(WIN):
            rows = pl.ds(w, 8, stride=PITCH)
            t = t_ref[unit, rows, :]
            total = s_ref[unit, rows, :]
            for j in range(STA):
                v = t * m_ref[kind * STA + j, rows, :]
                k23[j] = v if w == 0 else k23[j] + v
            for n in range(4):
                v = total * d_ref[kind * 4 + n, rows, :]
                k1[n] = v if w == 0 else k1[n] + v
        base = (unit if kind == 0 else unit + 1) * 64
        for n in range(4):
            lower, upper = spread_of(k1[n])
            values = [lower - k23[2 * n], upper - k23[2 * n + 1] if n < 3 else zero]
            x_ref[base + n * 16:base + (n + 1) * 16, :] = jnp.concatenate(values, axis=0).astype(BF16)
    total = part_ref[...] + jnp.dot(hot_ref[...], x_ref[...], preferred_element_type=F32)
    for w, tile in enumerate(chunk_transpose([total[k * 64:(k + 1) * 64, :] for k in range(CAP)])):
        out_ref[pl.ds(w, 64, stride=4), :] = tile


def finish_kernel(in_ref, out_ref, s_ref):
    total = in_ref[0]
    for z in range(1, 8):
        total = total + in_ref[z]
    s_ref[...] = total * (1.0 / 64.0)
    tiles = chunk_transpose([s_ref[pl.ds(m, 8, stride=4), :] for m in range(4)])
    for k in range(CAP):
        for t in range(8):
            out_ref[k:k + 1, t * LANES:(t + 1) * LANES] = tiles[k][t:t + 1, :]


def in_vmem(value):
    return pltpu.with_memory_space_constraint(value, pltpu.VMEM)


def on_device(spectra, pair_bins, owner_count, bin_order):
    vmem = pl.BlockSpec(memory_space=pltpu.VMEM)
    in_hbm = pl.BlockSpec(memory_space=pl.ANY)
    packed, counts, order = pl.pallas_call(
        pack_kernel,
        out_shape=(
            pltpu.VMEM((32, MSG, LANES), BF16),
            pltpu.VMEM((1, owner_count.shape[0]), jnp.int32),
            pltpu.VMEM((1, bin_order.shape[0]), jnp.int32),
        ),
        in_specs=[in_hbm] * 4,
        out_specs=(vmem,) * 3,
        scratch_shapes=[
            pltpu.VMEM((STA, WIN, 4096), BF16),
            pltpu.VMEM((ROUNDS, STA, STA), jnp.int32),
            pltpu.SemaphoreType.DMA((STA,)),
            pltpu.SemaphoreType.DMA((3,)),
        ],
        name="pack",
    )(
        jnp.transpose(spectra, (1, 0, 2)),
        jnp.transpose(pair_bins, (1, 0, 2)),
        owner_count.reshape(1, -1),
        bin_order.reshape(1, -1),
    )
    own = lax.all_to_all(packed, ("y", "c", "win"), 0, 0)
    count = lax.axis_size("z")
    halo = lax.ppermute(own[24:32, :ROWS], "z", [(i, (i + 1) % count) for i in range(count)])
    units = STA + 4
    between = pl.pallas_call(
        cross_kernel,
        out_shape=(
            pltpu.VMEM((256, LANES), F32),
            pltpu.VMEM((256, 6 * LANES), BF16),
            pltpu.VMEM((units, 8 * PITCH, LANES), F32),
            pltpu.VMEM((units, 8 * PITCH, LANES), F32),
        ),
        in_specs=[vmem] * 3,
        out_specs=(vmem,) * 4,
        scratch_shapes=[
            pltpu.VMEM((STA, 144, LANES), F32),
            pltpu.VMEM((STA, 144, LANES), F32),
            pltpu.VMEM((STA, 176, LANES), F32),
            pltpu.VMEM((STA, 144, LANES), F32),
            pltpu.VMEM((3, 144, LANES), F32),
            pltpu.VMEM((STA, 64, LANES), F32),
            pltpu.VMEM((STA * KI, NG * LANES), BF16),
            pltpu.VMEM((256, STA * KI), BF16),
        ],
        compiler_params=SMALL,
        name="cross",
    )(in_vmem(own), in_vmem(counts), in_vmem(order))
    send = pl.pallas_call(
        edge_kernel,
        out_shape=pltpu.VMEM((256, LANES), F32),
        in_specs=[vmem] * 5,
        out_specs=vmem,
        scratch_shapes=[
            pltpu.VMEM((2 * STA, 8 * PITCH, LANES), F32),
            pltpu.VMEM((8, 8 * PITCH, LANES), F32),
            pltpu.VMEM((6 * LANES, LANES), BF16),
        ],
        compiler_params=SMALL,
        name="edge",
    )(in_vmem(halo), *(in_vmem(v) for v in between))
    got = lax.all_to_all(send.reshape(256, 1, LANES), ("z", "y", "c", "win"), 0, 0)
    got = in_vmem(got.reshape(8, 32, LANES))
    return pl.pallas_call(
        finish_kernel,
        out_shape=jax.ShapeDtypeStruct((CAP, 1024), F32),
        in_specs=[vmem],
        out_specs=vmem,
        scratch_shapes=[pltpu.VMEM((32, LANES), F32)],
        compiler_params=SMALL,
        name="finish",
    )(got)


def solution(mesh):
    fine = Mesh(mesh.devices.reshape(8, 4, 2, 4), ("z", "y", "c", "win"))
    sta = ("z", "y", "c")
    return jax.shard_map(
        on_device,
        mesh=fine,
        in_specs=(P("win", sta, None), P(sta, None, None), P(), P()),
        out_specs=P(sta, "win"),
        check_vma=False,
    )
```

```python
import jax
import jax.numpy as jnp
from jax import lax
from jax.experimental import pallas as pl
from jax.experimental.pallas import tpu as pltpu
from jax.sharding import Mesh, PartitionSpec as P

PLANE = 8
STA = 7
WIN = 16
NG = 4
ROUNDS = 3
CAP = 4
ROWS = STA * WIN
MSG = ROWS + 8
PITCH = WIN + 1
LANES = 128
CHUNK = 32
KI = 256
SMALL = pltpu.CompilerParams(vmem_limit_bytes=16 << 20)
F32 = jnp.float32
BF16 = jnp.bfloat16


def lane_iota(shape):
    return lax.broadcasted_iota(jnp.int32, shape, len(shape) - 1)


def chunk_transpose(tiles):
    lane = lane_iota(tiles[0].shape)
    low = lane < 64
    even = (lane % 64) < CHUNK
    axis = tiles[0].ndim - 1

    def diagonals(a, b, c, d):
        ab, cd = jnp.where(even, a, b), jnp.where(even, c, d)
        bc, da = jnp.where(even, b, c), jnp.where(even, d, a)
        return jnp.where(low, ab, cd), jnp.where(low, bc, da), jnp.where(low, cd, ab), jnp.where(low, da, bc)

    g0, g1, g2, g3 = diagonals(*tiles)
    v0, v3, v2, v1 = diagonals(g0, *(pltpu.roll(g, k * CHUNK, axis) for k, g in ((1, g1), (2, g2), (3, g3))))
    return v0, v1, v2, v3


def pack_kernel(x_hbm, bins_hbm, count_hbm, order_hbm, out_ref, count_ref, order_ref, x_ref, bins_ref, sems, small_sems):
    def station(s):
        return pltpu.make_async_copy(x_hbm.at[s], x_ref.at[s], sems.at[s])

    bins_copy = pltpu.make_async_copy(bins_hbm, bins_ref, small_sems.at[0])
    count_copy = pltpu.make_async_copy(count_hbm, count_ref, small_sems.at[1])
    order_copy = pltpu.make_async_copy(order_hbm, order_ref, small_sems.at[2])
    bins_copy.start()
    for s in range(STA):
        station(s).start()
    count_copy.start()
    order_copy.start()
    bins_copy.wait()
    lane8 = lax.broadcasted_iota(jnp.int32, (STA, LANES), 1)
    row8 = lax.broadcasted_iota(jnp.int32, (STA, LANES), 0)
    labels = jnp.zeros((STA, LANES), F32)
    for r in range(ROUNDS):
        place = jnp.where(lane8 == row8 + 8 * r, 1.0, 0.0).astype(F32)
        labels = labels + jnp.dot(bins_ref[r].astype(F32), place, preferred_element_type=F32)
    labels = jnp.concatenate([labels, jnp.zeros((1, LANES), F32)], axis=0).astype(BF16)
    for d in range(32):
        out_ref[d, ROWS:MSG, :] = labels

    def step(s, carry):
        station(s).wait()
        rows = pl.ds(pl.multiple_of(s * WIN, WIN), WIN)
        for q in range(8):
            tiles = [x_ref[s, :, n * 1024 + q * LANES:n * 1024 + (q + 1) * LANES] for n in range(4)]
            for m, tile in enumerate(chunk_transpose(tiles)):
                out_ref[4 * q + m, rows, :] = tile
        return carry

    lax.fori_loop(0, STA, step, 0)
    count_copy.wait()
    order_copy.wait()


def slot_bins(count_ref, order_ref):
    row = lax.broadcasted_iota(jnp.int32, (64, 64), 0)
    lane = lax.broadcasted_iota(jnp.int32, (64, 64), 1)
    counts = jnp.broadcast_to(count_ref[...].astype(F32), (64, 64))
    start = jnp.sum(jnp.where(lane < row, counts, 0.0), axis=1, keepdims=True)
    count = jnp.sum(jnp.where(lane == row, counts, 0.0), axis=1, keepdims=True)
    lane = lax.broadcasted_iota(jnp.int32, (64, LANES), 1).astype(F32)
    order = jnp.broadcast_to(order_ref[...].astype(F32), (64, LANES))
    out = []
    for k in range(CAP):
        chosen = jnp.sum(jnp.where(lane == start + float(k), order, 0.0), axis=1, keepdims=True)
        out.append(jnp.where(count > float(k), chosen, -1.0))
    return out


def joined(p, q):
    low = lane_iota(p.shape) < 64
    return jnp.where(low, p, q) + pltpu.roll(jnp.where(low, q, p), 64, 1)


def spread_of(k):
    low = lane_iota(k.shape) < 64
    turned = pltpu.roll(k, 64, 1)
    return jnp.where(low, k, turned), jnp.where(low, turned, k)


def edge_labels(rows, first_round, second_round):
    col = lane_iota((LANES, LANES))
    row = lax.broadcasted_iota(jnp.int32, (LANES, LANES), 0)
    half, station = (col % 8) // 4, (col % 64) // 8
    out = []
    for part, (ref, value) in enumerate(((first_round, rows[0]), (second_round, rows[1]))):
        place = jnp.where((row == ref * 8 + station) & (half == part), 1.0, 0.0).astype(BF16)
        out.append(jnp.dot(value, place, preferred_element_type=F32))
    none = lax.broadcasted_iota(jnp.int32, (8, LANES), 0) == STA
    return jnp.where(none, -2.0, out[0] + out[1])


def partner_rows(m_ref, d_ref, piece, turned, mixed, there):
    low = lane_iota((WIN, LANES)) < 64
    for s in range(STA):
        m_ref[s, there, :] = mixed[s * WIN:(s + 1) * WIN]
    for n in range(4):
        s, t = 2 * n, min(2 * n + 1, STA - 1)
        d_ref[n, there, :] = jnp.where(low, piece[s * WIN:(s + 1) * WIN], turned[t * WIN:(t + 1) * WIN])


def cross_kernel(own_ref, count_ref, order_ref, out_ref, edge_hot_ref, edge_t_ref, edge_s_ref, edge_m_ref, edge_d_ref,
                 bins_ref, t_ref, s_ref, m_ref, e_ref, d_ref, f_ref, x_ref, hot_ref):
    lane = lane_iota((8, LANES))
    low = lane < 64
    zero = jnp.zeros((8, LANES), F32)

    spread = jnp.where(lax.broadcasted_iota(jnp.int32, (LANES, KI), 1) // 8
                       == lax.broadcasted_iota(jnp.int32, (LANES, KI), 0), 1.0, 0.0).astype(BF16)
    lane_q = lane_iota((8, KI))
    qmod = lane_q % 8
    labels = jnp.zeros((8, KI), F32)
    for b in range(PLANE):
        wide = jnp.dot(own_ref[b * NG, ROWS:MSG, :], spread, preferred_element_type=F32)
        labels = labels + jnp.where(qmod == b, wide, 0.0)
    labels = jnp.where(lane_q // 64 > qmod, -2.0, labels)
    rows_of = [labels[i:i + 1, h * LANES:(h + 1) * LANES] for i in range(STA) for h in range(2)]

    one = edge_labels((own_ref[0, ROWS:MSG, :], own_ref[NG, ROWS:MSG, :]), 1, 2)
    upper = lane_iota((1, LANES)) >= 64
    edge_rows = [jnp.where(upper, one[2 * p + 1:2 * p + 2], one[2 * p:2 * p + 1]) for p in range(4)]

    for k, column in enumerate(slot_bins(count_ref, order_ref)):
        bins = jnp.broadcast_to(column, (64, LANES))
        rows = slice(k * 64, (k + 1) * 64)
        bins_ref[rows, :] = bins
        for ref, line in ((hot_ref, rows_of), (edge_hot_ref, edge_rows)):
            for n, wanted in enumerate(line):
                ref[rows, n * LANES:(n + 1) * LANES] = jnp.where(
                    bins == jnp.broadcast_to(wanted, (64, LANES)), 1.0, 0.0).astype(BF16)

    for i in range(STA):
        f_ref[i, STA * 8:(STA + 1) * 8, :] = zero
        x_ref[i * KI + ROUNDS * 64:(i + 1) * KI, :] = jnp.zeros((64, NG * LANES), BF16)
        m_ref[i, 0:2 * PITCH, :] = jnp.zeros((2 * PITCH, LANES), F32)

    def per_shard(g, carry):
        low_rows = lane_iota((ROWS, LANES)) < 64
        before = [jnp.zeros((ROWS, LANES), F32)] * 2
        turned_before = jnp.zeros((ROWS, LANES), F32)
        for b in range(PLANE):
            piece = own_ref[b * NG + g, 0:ROWS, :].astype(F32)
            turned = pltpu.roll(piece, 64, 1)
            total = piece + turned
            mixed = jnp.where(low_rows, piece - turned, total)
            shared = jnp.where(low_rows, before[0], before[1])
            for s in range(STA):
                rows = slice(s * WIN, (s + 1) * WIN)
                own_rows = slice(b * PITCH, b * PITCH + WIN)
                t_ref[s, own_rows, :] = turned[rows]
                s_ref[s, own_rows, :] = total[rows]
                m_ref[s, (b + 2) * PITCH:(b + 2) * PITCH + WIN, :] = mixed[rows]
                e_ref[s, own_rows, :] = shared[rows]
                if s % 2 == 1:
                    d_ref[s // 2, own_rows, :] = jnp.where(
                        low_rows[:WIN], piece[rows], turned[(s + 1) * WIN:(s + 2) * WIN])
            if b < 2:
                for s in range(STA):
                    there = pl.ds((b * NG + g) * PITCH, WIN)
                    edge_t_ref[s, there, :] = turned[s * WIN:(s + 1) * WIN]
                    edge_s_ref[s, there, :] = total[s * WIN:(s + 1) * WIN]
            if b == PLANE - 2:
                for half in range(2):
                    partner_rows(edge_m_ref, edge_d_ref, piece, turned, mixed, pl.ds((half * NG + g) * PITCH, WIN))
            before = [piece, turned_before]
            turned_before = turned

        lanes = pl.ds(pl.multiple_of(g * LANES, LANES), LANES)

        def add(acc, key, w, v):
            acc[key] = v if w == 0 else acc[key] + v

        for i in range(STA):
            k1, k1_own, k23 = {}, {}, {}
            pairs = [n for n in range(3) if 2 * n + 2 > i]
            for w in range(WIN):
                rows = pl.ds(w, 8, stride=PITCH)
                t = t_ref[i, rows, :]
                total = s_ref[i, rows, :]
                add(k23, (0, i), w, t * t)
                for j in range(i + 1, STA):
                    add(k23, (0, j), w, t * m_ref[j, pl.ds(2 * PITCH + w, 8, stride=PITCH), :])
                for n in pairs:
                    add(k1_own, n, w, total * d_ref[n, rows, :])
            auto = k23[0, i]
            f_ref[i, i * 8:(i + 1) * 8, :] = jnp.where(low, auto + pltpu.roll(auto, 64, 1), 0.0)
            for n in pairs:
                for j, k in zip((2 * n + 1, 2 * n + 2), spread_of(k1_own[n])):
                    if j > i:
                        value = k - k23[0, j]
                        f_ref[i, j * 8:(j + 1) * 8, :] = value
                        f_ref[j, i * 8:(i + 1) * 8, :] = jnp.where(low, value, -value)
            for w in range(WIN):
                rows = pl.ds(w, 8, stride=PITCH)
                t = t_ref[i, rows, :]
                total = s_ref[i, rows, :]
                for j in range(STA):
                    add(k23, (1, j), w, t * m_ref[j, pl.ds(PITCH + w, 8, stride=PITCH), :])
                    add(k23, (2, j), w, t * m_ref[j, rows, :])
                    add(k1, j, w, total * e_ref[j, rows, :])
            values = {(1, STA): zero, (2, STA): zero}
            for j in range(STA):
                for r, k in zip((1, 2), spread_of(k1[j])):
                    values[r, j] = k - k23[r, j]
            for r in (1, 2):
                for j in range(0, 8, 2):
                    pair = jnp.concatenate([values[r, j], values[r, j + 1]], axis=0).astype(BF16)
                    base = i * KI + (r * 8 + j) * 8
                    x_ref[base:base + 16, lanes] = pair
        for i in range(STA):
            x_ref[i * KI:i * KI + 64, lanes] = f_ref[i].astype(BF16)
        return carry

    lax.fori_loop(0, NG, per_shard, 0)
    total = jnp.dot(hot_ref[...], x_ref[...], preferred_element_type=F32)
    out_ref[...] = (total[:, 0:128] + total[:, 128:256]) + (total[:, 256:384] + total[:, 384:512])


def edge_kernel(after_ref, before_ref, part_ref, hot_ref, t_ref, s_ref, own_m_ref, own_d_ref, bins_ref, out_ref,
                m_ref, d_ref, after_t_ref, after_s_ref, x_ref, after_hot_ref):
    low_rows = lane_iota((ROWS, LANES)) < 64
    zero = jnp.zeros((8, LANES), F32)
    for g in range(NG):
        piece = before_ref[g].astype(F32)
        turned = pltpu.roll(piece, 64, 1)
        mixed = jnp.where(low_rows, piece - turned, piece + turned)
        for half in range(2):
            base = (half * NG + g) * PITCH
            partner_rows(m_ref, d_ref, piece, turned, mixed, slice(base, base + WIN))
        piece = after_ref[g, 0:ROWS, :].astype(F32)
        turned = pltpu.roll(piece, 64, 1)
        total = piece + turned
        for n in range(8):
            s, base = min(n, STA - 1), ((n % 2) * NG + g) * PITCH
            after_t_ref[n // 2, base:base + WIN, :] = turned[s * WIN:(s + 1) * WIN]
            after_s_ref[n // 2, base:base + WIN, :] = total[s * WIN:(s + 1) * WIN]

    two = edge_labels((after_ref[0, ROWS:MSG, :],) * 2, 2, 2)
    lane_1 = lane_iota((1, LANES))
    upper, second_half = lane_1 >= 64, lane_1 % 8 >= 4
    for p in (0, 2):
        lower_unit = jnp.where(second_half, two[2 * p + 1:2 * p + 2], two[2 * p:2 * p + 1])
        upper_unit = jnp.where(second_half, two[2 * p + 3:2 * p + 4], two[2 * p + 2:2 * p + 3])
        wanted = jnp.broadcast_to(jnp.where(upper, upper_unit, lower_unit), (256, LANES))
        after_hot_ref[:, p * 64:p * 64 + LANES] = jnp.where(bins_ref[...] == wanted, 1.0, 0.0).astype(BF16)

    x_ref[3 * LANES + 64:4 * LANES, :] = jnp.zeros((64, LANES), BF16)
    for unit in range(STA + 4):
        here = unit < STA
        own_t, own_s, place = (t_ref, s_ref, unit) if here else (after_t_ref, after_s_ref, unit - STA)
        other_m, other_d = (m_ref, d_ref) if here else (own_m_ref, own_d_ref)
        k1, k23 = {}, {}
        for w in range(WIN):
            rows = pl.ds(w, 8, stride=PITCH)
            t = own_t[place, rows, :]
            total = own_s[place, rows, :]
            for j in range(STA):
                v = t * other_m[j, rows, :]
                k23[j] = v if w == 0 else k23[j] + v
            for n in range(4):
                v = total * other_d[n, rows, :]
                k1[n] = v if w == 0 else k1[n] + v
        base = (unit if here else unit + 1) * 64
        for n in range(4):
            lower, upper = spread_of(k1[n])
            values = [lower - k23[2 * n], upper - k23[2 * n + 1] if n < 3 else zero]
            x_ref[base + n * 16:base + (n + 1) * 16, :] = jnp.concatenate(values, axis=0).astype(BF16)
    total = part_ref[...] + jnp.dot(hot_ref[...], x_ref[0:4 * LANES, :], preferred_element_type=F32)
    total = total + jnp.dot(after_hot_ref[...], x_ref[4 * LANES:, :], preferred_element_type=F32)
    for w, tile in enumerate(chunk_transpose([total[k * 64:(k + 1) * 64, :] for k in range(CAP)])):
        out_ref[pl.ds(w, 64, stride=4), :] = tile


def finish_kernel(in_ref, out_ref, s_ref):
    total = in_ref[0]
    for z in range(1, 8):
        total = total + in_ref[z]
    s_ref[...] = total * (1.0 / 64.0)
    tiles = chunk_transpose([s_ref[pl.ds(m, 8, stride=4), :] for m in range(4)])
    for k in range(CAP):
        for t in range(8):
            out_ref[k:k + 1, t * LANES:(t + 1) * LANES] = tiles[k][t:t + 1, :]


def in_vmem(value):
    return pltpu.with_memory_space_constraint(value, pltpu.VMEM)


def on_device(spectra, pair_bins, owner_count, bin_order):
    vmem = pl.BlockSpec(memory_space=pltpu.VMEM)
    in_hbm = pl.BlockSpec(memory_space=pl.ANY)
    packed, counts, order = pl.pallas_call(
        pack_kernel,
        out_shape=(
            pltpu.VMEM((32, MSG, LANES), BF16),
            pltpu.VMEM((1, owner_count.shape[0]), jnp.int32),
            pltpu.VMEM((1, bin_order.shape[0]), jnp.int32),
        ),
        in_specs=[in_hbm] * 4,
        out_specs=(vmem,) * 3,
        scratch_shapes=[
            pltpu.VMEM((STA, WIN, 4096), BF16),
            pltpu.VMEM((ROUNDS, STA, STA), jnp.int32),
            pltpu.SemaphoreType.DMA((STA,)),
            pltpu.SemaphoreType.DMA((3,)),
        ],
        name="pack",
    )(
        jnp.transpose(spectra, (1, 0, 2)),
        jnp.transpose(pair_bins, (1, 0, 2)),
        owner_count.reshape(1, -1),
        bin_order.reshape(1, -1),
    )
    own = lax.all_to_all(packed, ("y", "c", "win"), 0, 0)
    count = lax.axis_size("z")
    before = lax.ppermute(own[28:32, :ROWS], "z", [(i, (i + 1) % count) for i in range(count)])
    after = lax.ppermute(own[0:4], "z", [((i + 1) % count, i) for i in range(count)])
    operand = pltpu.VMEM((STA, 8 * PITCH, LANES), F32)
    shared = pltpu.VMEM((4, 8 * PITCH, LANES), F32)
    between = pl.pallas_call(
        cross_kernel,
        out_shape=(
            pltpu.VMEM((256, LANES), F32),
            pltpu.VMEM((256, 4 * LANES), BF16),
            operand,
            operand,
            operand,
            shared,
            pltpu.VMEM((256, LANES), F32),
        ),
        in_specs=[vmem] * 3,
        out_specs=(vmem,) * 7,
        scratch_shapes=[
            pltpu.VMEM((STA, 144, LANES), F32),
            pltpu.VMEM((STA, 144, LANES), F32),
            pltpu.VMEM((STA, 176, LANES), F32),
            pltpu.VMEM((STA, 144, LANES), F32),
            pltpu.VMEM((3, 144, LANES), F32),
            pltpu.VMEM((STA, 64, LANES), F32),
            pltpu.VMEM((STA * KI, NG * LANES), BF16),
            pltpu.VMEM((256, STA * KI), BF16),
        ],
        compiler_params=SMALL,
        name="cross",
    )(in_vmem(own), in_vmem(counts), in_vmem(order))
    send = pl.pallas_call(
        edge_kernel,
        out_shape=pltpu.VMEM((256, LANES), F32),
        in_specs=[vmem] * 9,
        out_specs=vmem,
        scratch_shapes=[
            operand,
            shared,
            shared,
            shared,
            pltpu.VMEM((6 * LANES, LANES), BF16),
            pltpu.VMEM((256, 2 * LANES), BF16),
        ],
        compiler_params=SMALL,
        name="edge",
    )(in_vmem(after), in_vmem(before), *(in_vmem(v) for v in between))
    got = lax.all_to_all(send.reshape(256, 1, LANES), ("z", "y", "c", "win"), 0, 0)
    got = in_vmem(got.reshape(8, 32, LANES))
    return pl.pallas_call(
        finish_kernel,
        out_shape=jax.ShapeDtypeStruct((CAP, 1024), F32),
        in_specs=[vmem],
        out_specs=vmem,
        scratch_shapes=[pltpu.VMEM((32, LANES), F32)],
        compiler_params=SMALL,
        name="finish",
    )(got)


def solution(mesh):
    fine = Mesh(mesh.devices.reshape(8, 4, 2, 4), ("z", "y", "c", "win"))
    sta = ("z", "y", "c")
    return jax.shard_map(
        on_device,
        mesh=fine,
        in_specs=(P("win", sta, None), P(sta, None, None), P(), P()),
        out_specs=P(sta, "win"),
        check_vma=False,
    )
```

```python
import jax
import jax.numpy as jnp
from jax import lax
from jax.experimental import pallas as pl
from jax.experimental.pallas import tpu as pltpu
from jax.sharding import Mesh, PartitionSpec as P

PLANE = 8
STA = 7
WIN = 16
NG = 4
ROUNDS = 3
CAP = 4
ROWS = STA * WIN
MSG = ROWS + 8
PITCH = WIN + 1
LANES = 128
CHUNK = 32
KI = 256
SMALL = pltpu.CompilerParams(vmem_limit_bytes=16 << 20)
F32 = jnp.float32
BF16 = jnp.bfloat16


def lane_iota(shape):
    return lax.broadcasted_iota(jnp.int32, shape, len(shape) - 1)


def chunk_transpose(tiles):
    lane = lane_iota(tiles[0].shape)
    low = lane < 64
    even = (lane % 64) < CHUNK
    axis = tiles[0].ndim - 1

    def diagonals(a, b, c, d):
        ab, cd = jnp.where(even, a, b), jnp.where(even, c, d)
        bc, da = jnp.where(even, b, c), jnp.where(even, d, a)
        return jnp.where(low, ab, cd), jnp.where(low, bc, da), jnp.where(low, cd, ab), jnp.where(low, da, bc)

    g0, g1, g2, g3 = diagonals(*tiles)
    v0, v3, v2, v1 = diagonals(g0, *(pltpu.roll(g, k * CHUNK, axis) for k, g in ((1, g1), (2, g2), (3, g3))))
    return v0, v1, v2, v3


def pack_kernel(x_hbm, bins_hbm, count_hbm, order_hbm, out_ref, count_ref, order_ref, x_ref, bins_ref, sems, small_sems):
    def station(s):
        return pltpu.make_async_copy(x_hbm.at[s], x_ref.at[s], sems.at[s])

    bins_copy = pltpu.make_async_copy(bins_hbm, bins_ref, small_sems.at[0])
    count_copy = pltpu.make_async_copy(count_hbm, count_ref, small_sems.at[1])
    order_copy = pltpu.make_async_copy(order_hbm, order_ref, small_sems.at[2])
    bins_copy.start()
    for s in range(STA):
        station(s).start()
    count_copy.start()
    order_copy.start()
    bins_copy.wait()
    lane8 = lax.broadcasted_iota(jnp.int32, (STA, LANES), 1)
    row8 = lax.broadcasted_iota(jnp.int32, (STA, LANES), 0)
    labels = jnp.zeros((STA, LANES), F32)
    for r in range(ROUNDS):
        place = jnp.where(lane8 == row8 + 8 * r, 1.0, 0.0).astype(F32)
        labels = labels + jnp.dot(bins_ref[r].astype(F32), place, preferred_element_type=F32)
    labels = jnp.concatenate([labels, jnp.zeros((1, LANES), F32)], axis=0).astype(BF16)
    for d in range(32):
        out_ref[d, ROWS:MSG, :] = labels

    def step(s, carry):
        station(s).wait()
        rows = pl.ds(pl.multiple_of(s * WIN, WIN), WIN)
        for q in range(8):
            tiles = [x_ref[s, :, n * 1024 + q * LANES:n * 1024 + (q + 1) * LANES] for n in range(4)]
            for m, tile in enumerate(chunk_transpose(tiles)):
                out_ref[4 * q + m, rows, :] = tile
        return carry

    lax.fori_loop(0, STA, step, 0)
    count_copy.wait()
    order_copy.wait()


def positions(count_ref, order_ref):
    row = lax.broadcasted_iota(jnp.int32, (64, 64), 0)
    lane = lax.broadcasted_iota(jnp.int32, (64, 64), 1)
    counts = jnp.broadcast_to(count_ref[...].astype(F32), (64, 64))
    start = jnp.sum(jnp.where(lane < row, counts, 0.0), axis=1, keepdims=True)
    count = jnp.sum(jnp.where(lane == row, counts, 0.0), axis=1, keepdims=True)
    lane = lax.broadcasted_iota(jnp.int32, (64, LANES), 1).astype(F32)
    slots = [jnp.where((lane == start + float(k)) & (count > float(k)), 1.0, 0.0).astype(BF16) for k in range(CAP)]
    row = lax.broadcasted_iota(jnp.int32, (LANES, LANES), 0)
    lane = lax.broadcasted_iota(jnp.int32, (LANES, LANES), 1)
    order = jnp.broadcast_to(order_ref[...].astype(F32), (LANES, LANES))
    return jnp.sum(jnp.where(lane == row, order, 0.0), axis=1, keepdims=True), slots


def spread_of(k):
    low = lane_iota(k.shape) < 64
    turned = pltpu.roll(k, 64, 1)
    return jnp.where(low, k, turned), jnp.where(low, turned, k)


def edge_labels(rows, first_round, second_round):
    col = lane_iota((LANES, LANES))
    row = lax.broadcasted_iota(jnp.int32, (LANES, LANES), 0)
    half, station = (col % 8) // 4, (col % 64) // 8
    out = []
    for part, (ref, value) in enumerate(((first_round, rows[0]), (second_round, rows[1]))):
        place = jnp.where((row == ref * 8 + station) & (half == part), 1.0, 0.0).astype(BF16)
        out.append(jnp.dot(value, place, preferred_element_type=F32))
    none = lax.broadcasted_iota(jnp.int32, (8, LANES), 0) == STA
    return jnp.where(none, -2.0, out[0] + out[1])


def partner_rows(m_ref, d_ref, piece, turned, mixed, there):
    low = lane_iota((WIN, LANES)) < 64
    for s in range(STA):
        m_ref[s, there, :] = mixed[s * WIN:(s + 1) * WIN]
    for n in range(4):
        s, t = 2 * n, min(2 * n + 1, STA - 1)
        d_ref[n, there, :] = jnp.where(low, piece[s * WIN:(s + 1) * WIN], turned[t * WIN:(t + 1) * WIN])


def cross_kernel(own_ref, count_ref, order_ref, out_ref, edge_hot_ref, edge_t_ref, edge_s_ref, edge_m_ref, edge_d_ref,
                 bins_ref, slot_ref, *scratch):
    sets, x_ref, hot_ref = (scratch[0:6],), scratch[6], scratch[7]
    lane = lane_iota((8, LANES))
    low = lane < 64
    zero = jnp.zeros((8, LANES), F32)

    spread = jnp.where(lax.broadcasted_iota(jnp.int32, (LANES, KI), 1) // 8
                       == lax.broadcasted_iota(jnp.int32, (LANES, KI), 0), 1.0, 0.0).astype(BF16)
    lane_q = lane_iota((8, KI))
    qmod = lane_q % 8
    labels = jnp.zeros((8, KI), F32)
    for b in range(PLANE):
        wide = jnp.dot(own_ref[b * NG, ROWS:MSG, :], spread, preferred_element_type=F32)
        labels = labels + jnp.where(qmod == b, wide, 0.0)
    labels = jnp.where(lane_q // 64 > qmod, -2.0, labels)
    labels = labels.astype(BF16)
    rows_of = [labels[i:i + 1, h * LANES:(h + 1) * LANES] for i in range(STA) for h in range(2)]

    one = edge_labels((own_ref[0, ROWS:MSG, :], own_ref[NG, ROWS:MSG, :]), 1, 2)
    upper = lane_iota((1, LANES)) >= 64
    edge_rows = [jnp.where(upper, one[2 * p + 1:2 * p + 2], one[2 * p:2 * p + 1]) for p in range(4)]

    column, slots = positions(count_ref, order_ref)
    for k in range(CAP):
        slot_ref[k * 64:(k + 1) * 64, :] = slots[k]
    bins = jnp.broadcast_to(column, (LANES, LANES)).astype(BF16)
    bins_ref[...] = bins
    one_bf16, zero_bf16 = jnp.ones((LANES, LANES), BF16), jnp.zeros((LANES, LANES), BF16)
    for ref, line in ((hot_ref, rows_of), (edge_hot_ref, edge_rows)):
        for n, wanted in enumerate(line):
            ref[:, n * LANES:(n + 1) * LANES] = jnp.where(
                bins == jnp.broadcast_to(wanted.astype(BF16), (LANES, LANES)), one_bf16, zero_bf16)

    for i in range(STA):
        x_ref[i * KI + ROUNDS * 64:(i + 1) * KI, :] = jnp.zeros((64, NG * LANES), BF16)
        for _, _, m_ref, _, _, f_ref in sets:
            f_ref[i, STA * 8:(STA + 1) * 8, :] = zero
            m_ref[i, 0:2 * PITCH, :] = jnp.zeros((2 * PITCH, LANES), F32)

    def prepare(g, refs):
        t_ref, s_ref, m_ref, e_ref, d_ref, _ = refs
        low_rows = lane_iota((ROWS, LANES)) < 64
        before = [jnp.zeros((ROWS, LANES), F32)] * 2
        turned_before = jnp.zeros((ROWS, LANES), F32)
        for b in range(PLANE):
            piece = own_ref[b * NG + g, 0:ROWS, :].astype(F32)
            turned = pltpu.roll(piece, 64, 1)
            total = piece + turned
            mixed = jnp.where(low_rows, piece - turned, total)
            shared = jnp.where(low_rows, before[0], before[1])
            for s in range(STA):
                rows = slice(s * WIN, (s + 1) * WIN)
                own_rows = slice(b * PITCH, b * PITCH + WIN)
                t_ref[s, own_rows, :] = turned[rows]
                s_ref[s, own_rows, :] = total[rows]
                m_ref[s, (b + 2) * PITCH:(b + 2) * PITCH + WIN, :] = mixed[rows]
                e_ref[s, own_rows, :] = shared[rows]
                if s % 2 == 1:
                    d_ref[s // 2, own_rows, :] = jnp.where(
                        low_rows[:WIN], piece[rows], turned[(s + 1) * WIN:(s + 2) * WIN])
            if b < 2:
                for s in range(STA):
                    there = pl.ds((b * NG + g) * PITCH, WIN)
                    edge_t_ref[s, there, :] = turned[s * WIN:(s + 1) * WIN]
                    edge_s_ref[s, there, :] = total[s * WIN:(s + 1) * WIN]
            if b == PLANE - 2:
                for half in range(2):
                    partner_rows(edge_m_ref, edge_d_ref, piece, turned, mixed, pl.ds((half * NG + g) * PITCH, WIN))
            before = [piece, turned_before]
            turned_before = turned

    def compute(g, refs):
        t_ref, s_ref, m_ref, e_ref, d_ref, f_ref = refs
        lanes = pl.ds(pl.multiple_of(g * LANES, LANES), LANES)

        def add(acc, key, w, v):
            acc[key] = v if w == 0 else acc[key] + v

        for group in ((0, 1), (2, 3), (4, 5), (6,)):
            k1, k23 = {}, {}
            for w in range(WIN):
                rows = pl.ds(w, 8, stride=PITCH)
                t = {i: t_ref[i, rows, :] for i in group}
                total = {i: s_ref[i, rows, :] for i in group}
                for i in group:
                    add(k23, (i, i), w, t[i] * t[i])
                for j in range(group[0] + 1, STA):
                    mixed = m_ref[j, pl.ds(2 * PITCH + w, 8, stride=PITCH), :]
                    for i in group:
                        if i < j:
                            add(k23, (i, j), w, t[i] * mixed)
                for n in range(group[0] // 2, 3 if group[0] < 6 else 0):
                    shared = d_ref[n, rows, :]
                    for i in group:
                        if i < 2 * n + 2:
                            add(k1, (i, n), w, total[i] * shared)
            for i in group:
                auto = k23[i, i]
                f_ref[i, i * 8:(i + 1) * 8, :] = jnp.where(low, auto + pltpu.roll(auto, 64, 1), 0.0)
            for (i, n), k in k1.items():
                for j, part in zip((2 * n + 1, 2 * n + 2), spread_of(k)):
                    if j > i:
                        value = part - k23[i, j]
                        f_ref[i, j * 8:(j + 1) * 8, :] = value
                        f_ref[j, i * 8:(i + 1) * 8, :] = jnp.where(low, value, -value)
        for i in range(STA):
            k1, k23 = {}, {}
            for w in range(WIN):
                rows = pl.ds(w, 8, stride=PITCH)
                t = t_ref[i, rows, :]
                total = s_ref[i, rows, :]
                for j in range(STA):
                    add(k23, (1, j), w, t * m_ref[j, pl.ds(PITCH + w, 8, stride=PITCH), :])
                    add(k23, (2, j), w, t * m_ref[j, rows, :])
                    add(k1, j, w, total * e_ref[j, rows, :])
            values = {(1, STA): zero, (2, STA): zero}
            for j in range(STA):
                for r, k in zip((1, 2), spread_of(k1[j])):
                    values[r, j] = k - k23[r, j]
            for r in (1, 2):
                for j in range(0, 8, 2):
                    pair = jnp.concatenate([values[r, j], values[r, j + 1]], axis=0).astype(BF16)
                    base = i * KI + (r * 8 + j) * 8
                    x_ref[base:base + 16, lanes] = pair
        for i in range(STA):
            x_ref[i * KI:i * KI + 64, lanes] = f_ref[i].astype(BF16)

    def per_shard(g, carry):
        prepare(g, sets[0])
        compute(g, sets[0])
        return carry

    lax.fori_loop(0, NG, per_shard, 0)
    total = jnp.dot(hot_ref[...], x_ref[...], preferred_element_type=F32)
    out_ref[...] = (total[:, 0:128] + total[:, 128:256]) + (total[:, 256:384] + total[:, 384:512])


def edge_kernel(after_ref, before_ref, part_ref, hot_ref, t_ref, s_ref, own_m_ref, own_d_ref, bins_ref, slot_ref, out_ref,
                m_ref, d_ref, after_t_ref, after_s_ref, x_ref, after_hot_ref):
    low_rows = lane_iota((ROWS, LANES)) < 64
    zero = jnp.zeros((8, LANES), F32)
    for g in range(NG):
        piece = before_ref[g].astype(F32)
        turned = pltpu.roll(piece, 64, 1)
        mixed = jnp.where(low_rows, piece - turned, piece + turned)
        for half in range(2):
            base = (half * NG + g) * PITCH
            partner_rows(m_ref, d_ref, piece, turned, mixed, slice(base, base + WIN))
        piece = after_ref[g, 0:ROWS, :].astype(F32)
        turned = pltpu.roll(piece, 64, 1)
        total = piece + turned
        for n in range(8):
            s, base = min(n, STA - 1), ((n % 2) * NG + g) * PITCH
            after_t_ref[n // 2, base:base + WIN, :] = turned[s * WIN:(s + 1) * WIN]
            after_s_ref[n // 2, base:base + WIN, :] = total[s * WIN:(s + 1) * WIN]

    two = edge_labels((after_ref[0, ROWS:MSG, :],) * 2, 2, 2)
    lane_1 = lane_iota((1, LANES))
    upper, second_half = lane_1 >= 64, lane_1 % 8 >= 4
    for p in (0, 2):
        lower_unit = jnp.where(second_half, two[2 * p + 1:2 * p + 2], two[2 * p:2 * p + 1])
        upper_unit = jnp.where(second_half, two[2 * p + 3:2 * p + 4], two[2 * p + 2:2 * p + 3])
        wanted = jnp.broadcast_to(jnp.where(upper, upper_unit, lower_unit).astype(BF16), (LANES, LANES))
        after_hot_ref[:, p * 64:p * 64 + LANES] = jnp.where(
            bins_ref[...] == wanted, jnp.ones((LANES, LANES), BF16), jnp.zeros((LANES, LANES), BF16))

    x_ref[3 * LANES + 64:4 * LANES, :] = jnp.zeros((64, LANES), BF16)
    for unit in range(STA + 4):
        here = unit < STA
        own_t, own_s, place = (t_ref, s_ref, unit) if here else (after_t_ref, after_s_ref, unit - STA)
        other_m, other_d = (m_ref, d_ref) if here else (own_m_ref, own_d_ref)
        k1, k23 = {}, {}
        for w in range(WIN):
            rows = pl.ds(w, 8, stride=PITCH)
            t = own_t[place, rows, :]
            total = own_s[place, rows, :]
            for j in range(STA):
                v = t * other_m[j, rows, :]
                k23[j] = v if w == 0 else k23[j] + v
            for n in range(4):
                v = total * other_d[n, rows, :]
                k1[n] = v if w == 0 else k1[n] + v
        base = (unit if here else unit + 1) * 64
        for n in range(4):
            lower, upper = spread_of(k1[n])
            values = [lower - k23[2 * n], upper - k23[2 * n + 1] if n < 3 else zero]
            x_ref[base + n * 16:base + (n + 1) * 16, :] = jnp.concatenate(values, axis=0).astype(BF16)
    total = part_ref[...] + jnp.dot(hot_ref[...], x_ref[0:4 * LANES, :], preferred_element_type=F32)
    total = total + jnp.dot(after_hot_ref[...], x_ref[4 * LANES:, :], preferred_element_type=F32)
    parts = []
    for _ in range(3):
        parts.append(total.astype(BF16))
        total = total - parts[-1].astype(F32)
    total = jnp.dot(slot_ref[...], jnp.concatenate(parts, axis=1), preferred_element_type=F32)
    total = (total[:, 0:128] + total[:, 128:256]) + total[:, 256:384]
    for w, tile in enumerate(chunk_transpose([total[k * 64:(k + 1) * 64, :] for k in range(CAP)])):
        out_ref[pl.ds(w, 64, stride=4), :] = tile


def finish_kernel(in_ref, out_ref, s_ref):
    total = in_ref[0]
    for z in range(1, 8):
        total = total + in_ref[z]
    s_ref[...] = total * (1.0 / 64.0)
    tiles = chunk_transpose([s_ref[pl.ds(m, 8, stride=4), :] for m in range(4)])
    for k in range(CAP):
        for t in range(8):
            out_ref[k:k + 1, t * LANES:(t + 1) * LANES] = tiles[k][t:t + 1, :]


def in_vmem(value):
    return pltpu.with_memory_space_constraint(value, pltpu.VMEM)


def on_device(spectra, pair_bins, owner_count, bin_order):
    vmem = pl.BlockSpec(memory_space=pltpu.VMEM)
    in_hbm = pl.BlockSpec(memory_space=pl.ANY)
    packed, counts, order = pl.pallas_call(
        pack_kernel,
        out_shape=(
            pltpu.VMEM((32, MSG, LANES), BF16),
            pltpu.VMEM((1, owner_count.shape[0]), jnp.int32),
            pltpu.VMEM((1, bin_order.shape[0]), jnp.int32),
        ),
        in_specs=[in_hbm] * 4,
        out_specs=(vmem,) * 3,
        scratch_shapes=[
            pltpu.VMEM((STA, WIN, 4096), BF16),
            pltpu.VMEM((ROUNDS, STA, STA), jnp.int32),
            pltpu.SemaphoreType.DMA((STA,)),
            pltpu.SemaphoreType.DMA((3,)),
        ],
        name="pack",
    )(
        jnp.transpose(spectra, (1, 0, 2)),
        jnp.transpose(pair_bins, (1, 0, 2)),
        owner_count.reshape(1, -1),
        bin_order.reshape(1, -1),
    )
    own = lax.all_to_all(packed, ("y", "c", "win"), 0, 0)
    count = lax.axis_size("z")
    before = lax.ppermute(own[28:32, :ROWS], "z", [(i, (i + 1) % count) for i in range(count)])
    after = lax.ppermute(own[0:4], "z", [((i + 1) % count, i) for i in range(count)])
    operand = pltpu.VMEM((STA, 8 * PITCH, LANES), F32)
    shared = pltpu.VMEM((4, 8 * PITCH, LANES), F32)
    between = pl.pallas_call(
        cross_kernel,
        out_shape=(
            pltpu.VMEM((LANES, LANES), F32),
            pltpu.VMEM((LANES, 4 * LANES), BF16),
            operand,
            operand,
            operand,
            shared,
            pltpu.VMEM((LANES, LANES), BF16),
            pltpu.VMEM((256, LANES), BF16),
        ),
        in_specs=[vmem] * 3,
        out_specs=(vmem,) * 8,
        scratch_shapes=[
            *(pltpu.VMEM((count, rows, LANES), F32)
              for count, rows in ((STA, 144), (STA, 144), (STA, 176), (STA, 144), (3, 144), (STA, 64))),
            pltpu.VMEM((STA * KI, NG * LANES), BF16),
            pltpu.VMEM((LANES, STA * KI), BF16),
        ],
        compiler_params=SMALL,
        name="cross",
    )(in_vmem(own), in_vmem(counts), in_vmem(order))
    send = pl.pallas_call(
        edge_kernel,
        out_shape=pltpu.VMEM((256, LANES), F32),
        in_specs=[vmem] * 10,
        out_specs=vmem,
        scratch_shapes=[
            operand,
            shared,
            shared,
            shared,
            pltpu.VMEM((6 * LANES, LANES), BF16),
            pltpu.VMEM((LANES, 2 * LANES), BF16),
        ],
        compiler_params=SMALL,
        name="edge",
    )(in_vmem(after), in_vmem(before), *(in_vmem(v) for v in between))
    got = lax.all_to_all(send.reshape(256, 1, LANES), ("z", "y", "c", "win"), 0, 0)
    got = in_vmem(got.reshape(8, 32, LANES))
    return pl.pallas_call(
        finish_kernel,
        out_shape=jax.ShapeDtypeStruct((CAP, 1024), F32),
        in_specs=[vmem],
        out_specs=vmem,
        scratch_shapes=[pltpu.VMEM((32, LANES), F32)],
        compiler_params=SMALL,
        name="finish",
    )(got)


def solution(mesh):
    fine = Mesh(mesh.devices.reshape(8, 4, 2, 4), ("z", "y", "c", "win"))
    sta = ("z", "y", "c")
    return jax.shard_map(
        on_device,
        mesh=fine,
        in_specs=(P("win", sta, None), P(sta, None, None), P(), P()),
        out_specs=P(sta, "win"),
        check_vma=False,
    )
```

```python
import jax
import jax.numpy as jnp
from jax import lax
from jax.experimental import pallas as pl
from jax.experimental.pallas import tpu as pltpu
from jax.sharding import Mesh, PartitionSpec as P

PLANE = 8
STA = 7
WIN = 16
NG = 4
ROUNDS = 3
CAP = 4
ROWS = STA * WIN
MSG = ROWS + 8
PITCH = WIN + 1
LANES = 128
CHUNK = 32
KI = 256
SMALL = pltpu.CompilerParams(vmem_limit_bytes=16 << 20)
F32 = jnp.float32
BF16 = jnp.bfloat16


def lane_iota(shape):
    return lax.broadcasted_iota(jnp.int32, shape, len(shape) - 1)


def chunk_transpose(tiles):
    lane = lane_iota(tiles[0].shape)
    low = lane < 64
    even = (lane % 64) < CHUNK
    axis = tiles[0].ndim - 1

    def diagonals(a, b, c, d):
        ab, cd = jnp.where(even, a, b), jnp.where(even, c, d)
        bc, da = jnp.where(even, b, c), jnp.where(even, d, a)
        return jnp.where(low, ab, cd), jnp.where(low, bc, da), jnp.where(low, cd, ab), jnp.where(low, da, bc)

    g0, g1, g2, g3 = diagonals(*tiles)
    v0, v3, v2, v1 = diagonals(g0, *(pltpu.roll(g, k * CHUNK, axis) for k, g in ((1, g1), (2, g2), (3, g3))))
    return v0, v1, v2, v3


def pack_kernel(x_hbm, bins_hbm, count_hbm, order_hbm, out_ref, count_ref, order_ref, x_ref, bins_ref, sems, small_sems):
    def station(s):
        return pltpu.make_async_copy(x_hbm.at[s], x_ref.at[s], sems.at[s])

    bins_copy = pltpu.make_async_copy(bins_hbm, bins_ref, small_sems.at[0])
    count_copy = pltpu.make_async_copy(count_hbm, count_ref, small_sems.at[1])
    order_copy = pltpu.make_async_copy(order_hbm, order_ref, small_sems.at[2])
    bins_copy.start()
    for s in range(STA):
        station(s).start()
    count_copy.start()
    order_copy.start()
    bins_copy.wait()
    lane8 = lax.broadcasted_iota(jnp.int32, (STA, LANES), 1)
    row8 = lax.broadcasted_iota(jnp.int32, (STA, LANES), 0)
    labels = jnp.zeros((STA, LANES), F32)
    for r in range(ROUNDS):
        place = jnp.where(lane8 == row8 + 8 * r, 1.0, 0.0).astype(F32)
        labels = labels + jnp.dot(bins_ref[r].astype(F32), place, preferred_element_type=F32)
    labels = jnp.concatenate([labels, jnp.zeros((1, LANES), F32)], axis=0).astype(BF16)
    for d in range(32):
        out_ref[d, ROWS:MSG, :] = labels

    def step(s, carry):
        station(s).wait()
        rows = pl.ds(pl.multiple_of(s * WIN, WIN), WIN)
        for q in range(8):
            tiles = [x_ref[s, :, n * 1024 + q * LANES:n * 1024 + (q + 1) * LANES] for n in range(4)]
            for m, tile in enumerate(chunk_transpose(tiles)):
                out_ref[4 * q + m, rows, :] = tile
        return carry

    lax.fori_loop(0, STA, step, 0)
    count_copy.wait()
    order_copy.wait()


def positions(count_ref, order_ref):
    row = lax.broadcasted_iota(jnp.int32, (64, 64), 0)
    lane = lax.broadcasted_iota(jnp.int32, (64, 64), 1)
    counts = jnp.broadcast_to(count_ref[...].astype(F32), (64, 64))
    start = jnp.sum(jnp.where(lane < row, counts, 0.0), axis=1, keepdims=True)
    count = jnp.sum(jnp.where(lane == row, counts, 0.0), axis=1, keepdims=True)
    lane = lax.broadcasted_iota(jnp.int32, (64, LANES), 1).astype(F32)
    slots = [jnp.where((lane == start + float(k)) & (count > float(k)), 1.0, 0.0).astype(BF16) for k in range(CAP)]
    row = lax.broadcasted_iota(jnp.int32, (LANES, LANES), 0)
    lane = lax.broadcasted_iota(jnp.int32, (LANES, LANES), 1)
    order = jnp.broadcast_to(order_ref[...].astype(F32), (LANES, LANES))
    return jnp.sum(jnp.where(lane == row, order, 0.0), axis=1, keepdims=True), slots


def spread_of(k):
    low = lane_iota(k.shape) < 64
    turned = pltpu.roll(k, 64, 1)
    return jnp.where(low, k, turned), jnp.where(low, turned, k)


def edge_labels(rows, first_round, second_round):
    col = lane_iota((LANES, LANES))
    row = lax.broadcasted_iota(jnp.int32, (LANES, LANES), 0)
    half, station = (col % 8) // 4, (col % 64) // 8
    out = []
    for part, (ref, value) in enumerate(((first_round, rows[0]), (second_round, rows[1]))):
        place = jnp.where((row == ref * 8 + station) & (half == part), 1.0, 0.0).astype(BF16)
        out.append(jnp.dot(value, place, preferred_element_type=F32))
    none = lax.broadcasted_iota(jnp.int32, (8, LANES), 0) == STA
    return jnp.where(none, -2.0, out[0] + out[1])


def partner_rows(m_ref, d_ref, piece, turned, mixed, there):
    low = lane_iota((WIN, LANES)) < 64
    for s in range(STA):
        m_ref[s, there, :] = mixed[s * WIN:(s + 1) * WIN]
    for n in range(4):
        s, t = 2 * n, min(2 * n + 1, STA - 1)
        d_ref[n, there, :] = jnp.where(low, piece[s * WIN:(s + 1) * WIN], turned[t * WIN:(t + 1) * WIN])


def cross_kernel(own_ref, count_ref, order_ref, out_ref, edge_hot_ref, edge_t_ref, edge_s_ref, edge_m_ref, edge_d_ref,
                 bins_ref, slot_ref, *scratch):
    sets, x_ref, hot_ref = (scratch[0:6],), scratch[6], scratch[7]
    lane = lane_iota((8, LANES))
    low = lane < 64
    zero = jnp.zeros((8, LANES), F32)

    spread = jnp.where(lax.broadcasted_iota(jnp.int32, (LANES, KI), 1) // 8
                       == lax.broadcasted_iota(jnp.int32, (LANES, KI), 0), 1.0, 0.0).astype(BF16)
    lane_q = lane_iota((8, KI))
    qmod = lane_q % 8
    labels = jnp.zeros((8, KI), F32)
    for b in range(PLANE):
        wide = jnp.dot(own_ref[b * NG, ROWS:MSG, :], spread, preferred_element_type=F32)
        labels = labels + jnp.where(qmod == b, wide, 0.0)
    labels = jnp.where(lane_q // 64 > qmod, -2.0, labels)
    labels = labels.astype(BF16)
    rows_of = [labels[i:i + 1, h * LANES:(h + 1) * LANES] for i in range(STA) for h in range(2)]

    one = edge_labels((own_ref[0, ROWS:MSG, :], own_ref[NG, ROWS:MSG, :]), 1, 2)
    upper = lane_iota((1, LANES)) >= 64
    edge_rows = [jnp.where(upper, one[2 * p + 1:2 * p + 2], one[2 * p:2 * p + 1]) for p in range(4)]

    column, slots = positions(count_ref, order_ref)
    for k in range(CAP):
        slot_ref[k * 64:(k + 1) * 64, :] = slots[k]
    bins = jnp.broadcast_to(column, (LANES, LANES)).astype(BF16)
    bins_ref[...] = bins
    one_bf16, zero_bf16 = jnp.ones((LANES, LANES), BF16), jnp.zeros((LANES, LANES), BF16)
    for ref, line in ((hot_ref, rows_of), (edge_hot_ref, edge_rows)):
        for n, wanted in enumerate(line):
            ref[:, n * LANES:(n + 1) * LANES] = jnp.where(
                bins == jnp.broadcast_to(wanted.astype(BF16), (LANES, LANES)), one_bf16, zero_bf16)

    for i in range(STA):
        x_ref[i * KI + ROUNDS * 64:(i + 1) * KI, :] = jnp.zeros((64, NG * LANES), BF16)
        for _, _, m_ref, _, _, f_ref in sets:
            f_ref[i, STA * 8:(STA + 1) * 8, :] = zero
            m_ref[i, 0:2 * PITCH, :] = jnp.zeros((2 * PITCH, LANES), F32)

    def prepare(g, refs):
        t_ref, s_ref, m_ref, e_ref, d_ref, _ = refs
        low_rows = lane_iota((ROWS, LANES)) < 64
        before = [jnp.zeros((ROWS, LANES), F32)] * 2
        turned_before = jnp.zeros((ROWS, LANES), F32)
        for b in range(PLANE):
            piece = own_ref[b * NG + g, 0:ROWS, :].astype(F32)
            turned = pltpu.roll(piece, 64, 1)
            total = piece + turned
            mixed = jnp.where(low_rows, piece - turned, total)
            shared = jnp.where(low_rows, before[0], before[1])
            for s in range(STA):
                rows = slice(s * WIN, (s + 1) * WIN)
                own_rows = slice(b * PITCH, b * PITCH + WIN)
                t_ref[s, own_rows, :] = turned[rows]
                s_ref[s, own_rows, :] = total[rows]
                m_ref[s, (b + 2) * PITCH:(b + 2) * PITCH + WIN, :] = mixed[rows]
                e_ref[s, own_rows, :] = shared[rows]
                if s % 2 == 1:
                    d_ref[s // 2, own_rows, :] = jnp.where(
                        low_rows[:WIN], piece[rows], turned[(s + 1) * WIN:(s + 2) * WIN])
            if b < 2:
                for s in range(STA):
                    there = pl.ds((b * NG + g) * PITCH, WIN)
                    edge_t_ref[s, there, :] = turned[s * WIN:(s + 1) * WIN]
                    edge_s_ref[s, there, :] = total[s * WIN:(s + 1) * WIN]
            if b == PLANE - 2:
                for half in range(2):
                    partner_rows(edge_m_ref, edge_d_ref, piece, turned, mixed, pl.ds((half * NG + g) * PITCH, WIN))
            before = [piece, turned_before]
            turned_before = turned

    def compute(g, refs):
        t_ref, s_ref, m_ref, e_ref, d_ref, f_ref = refs
        lanes = pl.ds(pl.multiple_of(g * LANES, LANES), LANES)

        def add(acc, key, w, v):
            acc[key] = v if w == 0 else acc[key] + v

        for group in ((0, 1), (2, 3), (4, 5), (6,)):
            k1, k23 = {}, {}
            for w in range(WIN):
                rows = pl.ds(w, 8, stride=PITCH)
                t = {i: t_ref[i, rows, :] for i in group}
                total = {i: s_ref[i, rows, :] for i in group}
                for i in group:
                    add(k23, (i, i), w, t[i] * t[i])
                for j in range(group[0] + 1, STA):
                    mixed = m_ref[j, pl.ds(2 * PITCH + w, 8, stride=PITCH), :]
                    for i in group:
                        if i < j:
                            add(k23, (i, j), w, t[i] * mixed)
                for n in range(group[0] // 2, 3 if group[0] < 6 else 0):
                    shared = d_ref[n, rows, :]
                    for i in group:
                        if i < 2 * n + 2:
                            add(k1, (i, n), w, total[i] * shared)
            for i in group:
                auto = k23[i, i]
                f_ref[i, i * 8:(i + 1) * 8, :] = jnp.where(low, auto + pltpu.roll(auto, 64, 1), 0.0)
            for (i, n), k in k1.items():
                for j, part in zip((2 * n + 1, 2 * n + 2), spread_of(k)):
                    if j > i:
                        value = part - k23[i, j]
                        f_ref[i, j * 8:(j + 1) * 8, :] = value
                        f_ref[j, i * 8:(i + 1) * 8, :] = jnp.where(low, value, -value)
        for i in range(STA):
            k1, k23 = {}, {}
            for w in range(WIN):
                rows = pl.ds(w, 8, stride=PITCH)
                t = t_ref[i, rows, :]
                total = s_ref[i, rows, :]
                for j in range(STA):
                    add(k23, (1, j), w, t * m_ref[j, pl.ds(PITCH + w, 8, stride=PITCH), :])
                    add(k23, (2, j), w, t * m_ref[j, rows, :])
                    add(k1, j, w, total * e_ref[j, rows, :])
            values = {(1, STA): zero, (2, STA): zero}
            for j in range(STA):
                for r, k in zip((1, 2), spread_of(k1[j])):
                    values[r, j] = k - k23[r, j]
            for r in (1, 2):
                for j in range(0, 8, 2):
                    pair = jnp.concatenate([values[r, j], values[r, j + 1]], axis=0).astype(BF16)
                    base = i * KI + (r * 8 + j) * 8
                    x_ref[base:base + 16, lanes] = pair
        for i in range(STA):
            x_ref[i * KI:i * KI + 64, lanes] = f_ref[i].astype(BF16)

    def per_shard(g, carry):
        prepare(g, sets[0])
        compute(g, sets[0])
        return carry

    lax.fori_loop(0, NG, per_shard, 0)
    total = jnp.dot(hot_ref[...], x_ref[...], preferred_element_type=F32)
    out_ref[...] = (total[:, 0:128] + total[:, 128:256]) + (total[:, 256:384] + total[:, 384:512])


def edge_kernel(after_ref, before_ref, part_ref, hot_ref, t_ref, s_ref, own_m_ref, own_d_ref, bins_ref, slot_ref, out_ref,
                m_ref, d_ref, after_t_ref, after_s_ref, x_ref, after_hot_ref):
    low_rows = lane_iota((ROWS, LANES)) < 64
    zero = jnp.zeros((8, LANES), F32)
    for g in range(NG):
        piece = before_ref[g].astype(F32)
        turned = pltpu.roll(piece, 64, 1)
        mixed = jnp.where(low_rows, piece - turned, piece + turned)
        for half in range(2):
            base = (half * NG + g) * PITCH
            partner_rows(m_ref, d_ref, piece, turned, mixed, slice(base, base + WIN))
        piece = after_ref[g, 0:ROWS, :].astype(F32)
        turned = pltpu.roll(piece, 64, 1)
        total = piece + turned
        for n in range(8):
            s, base = min(n, STA - 1), ((n % 2) * NG + g) * PITCH
            after_t_ref[n // 2, base:base + WIN, :] = turned[s * WIN:(s + 1) * WIN]
            after_s_ref[n // 2, base:base + WIN, :] = total[s * WIN:(s + 1) * WIN]

    two = edge_labels((after_ref[0, ROWS:MSG, :],) * 2, 2, 2)
    lane_1 = lane_iota((1, LANES))
    upper, second_half = lane_1 >= 64, lane_1 % 8 >= 4
    for p in (0, 2):
        lower_unit = jnp.where(second_half, two[2 * p + 1:2 * p + 2], two[2 * p:2 * p + 1])
        upper_unit = jnp.where(second_half, two[2 * p + 3:2 * p + 4], two[2 * p + 2:2 * p + 3])
        wanted = jnp.broadcast_to(jnp.where(upper, upper_unit, lower_unit).astype(BF16), (LANES, LANES))
        after_hot_ref[:, p * 64:p * 64 + LANES] = jnp.where(
            bins_ref[...] == wanted, jnp.ones((LANES, LANES), BF16), jnp.zeros((LANES, LANES), BF16))

    x_ref[3 * LANES + 64:4 * LANES, :] = jnp.zeros((64, LANES), BF16)
    def products(own_t, own_s, place, other_m, other_d, base):
        k1, k23 = {}, {}
        for w in range(WIN):
            rows = pl.ds(w, 8, stride=PITCH)
            t = own_t[place, rows, :]
            total = own_s[place, rows, :]
            for j in range(STA):
                v = t * other_m[j, rows, :]
                k23[j] = v if w == 0 else k23[j] + v
            for n in range(4):
                v = total * other_d[n, rows, :]
                k1[n] = v if w == 0 else k1[n] + v
        for n in range(4):
            lower, upper = spread_of(k1[n])
            values = [lower - k23[2 * n], upper - k23[2 * n + 1] if n < 3 else zero]
            x_ref[pl.ds(base + n * 16, 16), :] = jnp.concatenate(values, axis=0).astype(BF16)

    def unit_pair(n, carry):
        products(t_ref, s_ref, n, m_ref, d_ref, pl.multiple_of(n * 64, 64))
        products(after_t_ref, after_s_ref, n, own_m_ref, own_d_ref, pl.multiple_of(4 * LANES + n * 64, 64))
        return carry

    lax.fori_loop(0, 4, unit_pair, 0)
    for unit in range(4, STA):
        products(t_ref, s_ref, unit, m_ref, d_ref, unit * 64)
    total = part_ref[...] + jnp.dot(hot_ref[...], x_ref[0:4 * LANES, :], preferred_element_type=F32)
    total = total + jnp.dot(after_hot_ref[...], x_ref[4 * LANES:, :], preferred_element_type=F32)
    parts = []
    for _ in range(3):
        parts.append(total.astype(BF16))
        total = total - parts[-1].astype(F32)
    total = jnp.dot(slot_ref[...], jnp.concatenate(parts, axis=1), preferred_element_type=F32)
    total = (total[:, 0:128] + total[:, 128:256]) + total[:, 256:384]
    for w, tile in enumerate(chunk_transpose([total[k * 64:(k + 1) * 64, :] for k in range(CAP)])):
        out_ref[pl.ds(w, 64, stride=4), :] = tile


def finish_kernel(in_ref, out_ref, s_ref):
    total = in_ref[0]
    for z in range(1, 8):
        total = total + in_ref[z]
    s_ref[...] = total * (1.0 / 64.0)
    tiles = chunk_transpose([s_ref[pl.ds(m, 8, stride=4), :] for m in range(4)])
    for k in range(CAP):
        for t in range(8):
            out_ref[k:k + 1, t * LANES:(t + 1) * LANES] = tiles[k][t:t + 1, :]


def in_vmem(value):
    return pltpu.with_memory_space_constraint(value, pltpu.VMEM)


def on_device(spectra, pair_bins, owner_count, bin_order):
    vmem = pl.BlockSpec(memory_space=pltpu.VMEM)
    in_hbm = pl.BlockSpec(memory_space=pl.ANY)
    packed, counts, order = pl.pallas_call(
        pack_kernel,
        out_shape=(
            pltpu.VMEM((32, MSG, LANES), BF16),
            pltpu.VMEM((1, owner_count.shape[0]), jnp.int32),
            pltpu.VMEM((1, bin_order.shape[0]), jnp.int32),
        ),
        in_specs=[in_hbm] * 4,
        out_specs=(vmem,) * 3,
        scratch_shapes=[
            pltpu.VMEM((STA, WIN, 4096), BF16),
            pltpu.VMEM((ROUNDS, STA, STA), jnp.int32),
            pltpu.SemaphoreType.DMA((STA,)),
            pltpu.SemaphoreType.DMA((3,)),
        ],
        name="pack",
    )(
        jnp.transpose(spectra, (1, 0, 2)),
        jnp.transpose(pair_bins, (1, 0, 2)),
        owner_count.reshape(1, -1),
        bin_order.reshape(1, -1),
    )
    own = lax.all_to_all(packed, ("y", "c", "win"), 0, 0)
    count = lax.axis_size("z")
    before = lax.ppermute(own[28:32, :ROWS], "z", [(i, (i + 1) % count) for i in range(count)])
    after = lax.ppermute(own[0:4], "z", [((i + 1) % count, i) for i in range(count)])
    operand = pltpu.VMEM((STA, 8 * PITCH, LANES), F32)
    shared = pltpu.VMEM((4, 8 * PITCH, LANES), F32)
    between = pl.pallas_call(
        cross_kernel,
        out_shape=(
            pltpu.VMEM((LANES, LANES), F32),
            pltpu.VMEM((LANES, 4 * LANES), BF16),
            operand,
            operand,
            operand,
            shared,
            pltpu.VMEM((LANES, LANES), BF16),
            pltpu.VMEM((256, LANES), BF16),
        ),
        in_specs=[vmem] * 3,
        out_specs=(vmem,) * 8,
        scratch_shapes=[
            *(pltpu.VMEM((count, rows, LANES), F32)
              for count, rows in ((STA, 144), (STA, 144), (STA, 176), (STA, 144), (3, 144), (STA, 64))),
            pltpu.VMEM((STA * KI, NG * LANES), BF16),
            pltpu.VMEM((LANES, STA * KI), BF16),
        ],
        compiler_params=SMALL,
        name="cross",
    )(in_vmem(own), in_vmem(counts), in_vmem(order))
    send = pl.pallas_call(
        edge_kernel,
        out_shape=pltpu.VMEM((256, LANES), F32),
        in_specs=[vmem] * 10,
        out_specs=vmem,
        scratch_shapes=[
            operand,
            shared,
            shared,
            shared,
            pltpu.VMEM((6 * LANES, LANES), BF16),
            pltpu.VMEM((LANES, 2 * LANES), BF16),
        ],
        compiler_params=SMALL,
        name="edge",
    )(in_vmem(after), in_vmem(before), *(in_vmem(v) for v in between))
    got = lax.all_to_all(send.reshape(256, 1, LANES), ("z", "y", "c", "win"), 0, 0)
    got = in_vmem(got.reshape(8, 32, LANES))
    return pl.pallas_call(
        finish_kernel,
        out_shape=jax.ShapeDtypeStruct((CAP, 1024), F32),
        in_specs=[vmem],
        out_specs=vmem,
        scratch_shapes=[pltpu.VMEM((32, LANES), F32)],
        compiler_params=SMALL,
        name="finish",
    )(got)


def solution(mesh):
    fine = Mesh(mesh.devices.reshape(8, 4, 2, 4), ("z", "y", "c", "win"))
    sta = ("z", "y", "c")
    return jax.shard_map(
        on_device,
        mesh=fine,
        in_specs=(P("win", sta, None), P(sta, None, None), P(), P()),
        out_specs=P(sta, "win"),
        check_vma=False,
    )
```

```python
import jax
import jax.numpy as jnp
from jax import lax
from jax.experimental import pallas as pl
from jax.experimental.pallas import tpu as pltpu
from jax.sharding import Mesh, PartitionSpec as P

PLANE = 8
STA = 7
WIN = 16
NG = 4
ROUNDS = 3
CAP = 4
ROWS = STA * WIN
MSG = ROWS + 8
PITCH = WIN + 1
LANES = 128
CHUNK = 32
KI = 256
SMALL = pltpu.CompilerParams(vmem_limit_bytes=16 << 20)
F32 = jnp.float32
BF16 = jnp.bfloat16


def lane_iota(shape):
    return lax.broadcasted_iota(jnp.int32, shape, len(shape) - 1)


def chunk_transpose(tiles):
    lane = lane_iota(tiles[0].shape)
    low = lane < 64
    even = (lane % 64) < CHUNK
    axis = tiles[0].ndim - 1

    def diagonals(a, b, c, d):
        ab, cd = jnp.where(even, a, b), jnp.where(even, c, d)
        bc, da = jnp.where(even, b, c), jnp.where(even, d, a)
        return jnp.where(low, ab, cd), jnp.where(low, bc, da), jnp.where(low, cd, ab), jnp.where(low, da, bc)

    g0, g1, g2, g3 = diagonals(*tiles)
    v0, v3, v2, v1 = diagonals(g0, *(pltpu.roll(g, k * CHUNK, axis) for k, g in ((1, g1), (2, g2), (3, g3))))
    return v0, v1, v2, v3


def pack_kernel(x_hbm, bins_hbm, count_hbm, order_hbm, out_ref, count_ref, order_ref, x_ref, bins_ref, sems, small_sems):
    def station(s):
        return pltpu.make_async_copy(x_hbm.at[s], x_ref.at[s], sems.at[s])

    bins_copy = pltpu.make_async_copy(bins_hbm, bins_ref, small_sems.at[0])
    count_copy = pltpu.make_async_copy(count_hbm, count_ref, small_sems.at[1])
    order_copy = pltpu.make_async_copy(order_hbm, order_ref, small_sems.at[2])
    bins_copy.start()
    for s in range(STA):
        station(s).start()
    count_copy.start()
    order_copy.start()
    bins_copy.wait()
    lane8 = lax.broadcasted_iota(jnp.int32, (STA, LANES), 1)
    row8 = lax.broadcasted_iota(jnp.int32, (STA, LANES), 0)
    labels = jnp.zeros((STA, LANES), F32)
    for r in range(ROUNDS):
        place = jnp.where(lane8 == row8 + 8 * r, 1.0, 0.0).astype(BF16)
        labels = labels + jnp.dot(bins_ref[r].astype(F32).astype(BF16), place, preferred_element_type=F32)
    labels = jnp.concatenate([labels, jnp.zeros((1, LANES), F32)], axis=0).astype(BF16)
    for d in range(32):
        out_ref[d, ROWS:MSG, :] = labels

    def step(s, carry):
        station(s).wait()
        rows = pl.ds(pl.multiple_of(s * WIN, WIN), WIN)
        for q in range(8):
            tiles = [x_ref[s, :, n * 1024 + q * LANES:n * 1024 + (q + 1) * LANES] for n in range(4)]
            for m, tile in enumerate(chunk_transpose(tiles)):
                out_ref[4 * q + m, rows, :] = tile
        return carry

    lax.fori_loop(0, STA, step, 0)
    count_copy.wait()
    order_copy.wait()


def positions(count_ref, order_ref):
    row = lax.broadcasted_iota(jnp.int32, (64, 64), 0)
    lane = lax.broadcasted_iota(jnp.int32, (64, 64), 1)
    counts = jnp.broadcast_to(count_ref[...].astype(F32), (64, 64))
    start = jnp.sum(jnp.where(lane < row, counts, 0.0), axis=1, keepdims=True)
    count = jnp.sum(jnp.where(lane == row, counts, 0.0), axis=1, keepdims=True)
    lane = lax.broadcasted_iota(jnp.int32, (64, LANES), 1).astype(F32)
    slots = [jnp.where((lane == start + float(k)) & (count > float(k)), 1.0, 0.0).astype(BF16) for k in range(CAP)]
    row = lax.broadcasted_iota(jnp.int32, (LANES, LANES), 0)
    lane = lax.broadcasted_iota(jnp.int32, (LANES, LANES), 1)
    order = jnp.broadcast_to(order_ref[...].astype(F32), (LANES, LANES))
    return jnp.sum(jnp.where(lane == row, order, 0.0), axis=1, keepdims=True), slots


def spread_of(k):
    low = lane_iota(k.shape) < 64
    turned = pltpu.roll(k, 64, 1)
    return jnp.where(low, k, turned), jnp.where(low, turned, k)


def edge_labels(rows, first_round, second_round):
    col = lane_iota((LANES, LANES))
    row = lax.broadcasted_iota(jnp.int32, (LANES, LANES), 0)
    half, station = (col % 8) // 4, (col % 64) // 8
    out = []
    for part, (ref, value) in enumerate(((first_round, rows[0]), (second_round, rows[1]))):
        place = jnp.where((row == ref * 8 + station) & (half == part), 1.0, 0.0).astype(BF16)
        out.append(jnp.dot(value, place, preferred_element_type=F32))
    none = lax.broadcasted_iota(jnp.int32, (8, LANES), 0) == STA
    return jnp.where(none, -2.0, out[0] + out[1])


def partner_rows(m_ref, d_ref, piece, turned, mixed, there):
    low = lane_iota((WIN, LANES)) < 64
    for s in range(STA):
        m_ref[s, there, :] = mixed[s * WIN:(s + 1) * WIN]
    for n in range(4):
        s, t = 2 * n, min(2 * n + 1, STA - 1)
        d_ref[n, there, :] = jnp.where(low, piece[s * WIN:(s + 1) * WIN], turned[t * WIN:(t + 1) * WIN])


def cross_kernel(own_ref, count_ref, order_ref, out_ref, edge_hot_ref, edge_t_ref, edge_s_ref, edge_m_ref, edge_d_ref,
                 bins_ref, slot_ref, *scratch):
    sets, x_ref, hot_ref = (scratch[0:6],), scratch[6], scratch[7]
    lane = lane_iota((8, LANES))
    low = lane < 64
    zero = jnp.zeros((8, LANES), F32)

    spread = jnp.where(lax.broadcasted_iota(jnp.int32, (LANES, KI), 1) // 8
                       == lax.broadcasted_iota(jnp.int32, (LANES, KI), 0), 1.0, 0.0).astype(BF16)
    lane_q = lane_iota((8, KI))
    qmod = lane_q % 8
    labels = jnp.zeros((8, KI), F32)
    for b in range(PLANE):
        wide = jnp.dot(own_ref[b * NG, ROWS:MSG, :], spread, preferred_element_type=F32)
        labels = labels + jnp.where(qmod == b, wide, 0.0)
    labels = jnp.where(lane_q // 64 > qmod, -2.0, labels)
    labels = labels.astype(BF16)
    rows_of = [labels[i:i + 1, h * LANES:(h + 1) * LANES] for i in range(STA) for h in range(2)]

    one = edge_labels((own_ref[0, ROWS:MSG, :], own_ref[NG, ROWS:MSG, :]), 1, 2)
    upper = lane_iota((1, LANES)) >= 64
    edge_rows = [jnp.where(upper, one[2 * p + 1:2 * p + 2], one[2 * p:2 * p + 1]) for p in range(4)]

    column, slots = positions(count_ref, order_ref)
    for k in range(CAP):
        slot_ref[k * 64:(k + 1) * 64, :] = slots[k]
    bins = jnp.broadcast_to(column, (LANES, LANES)).astype(BF16)
    bins_ref[...] = bins
    one_bf16, zero_bf16 = jnp.ones((LANES, LANES), BF16), jnp.zeros((LANES, LANES), BF16)
    for ref, line in ((hot_ref, rows_of), (edge_hot_ref, edge_rows)):
        for n, wanted in enumerate(line):
            ref[:, n * LANES:(n + 1) * LANES] = jnp.where(
                bins == jnp.broadcast_to(wanted.astype(BF16), (LANES, LANES)), one_bf16, zero_bf16)

    for i in range(STA):
        x_ref[i * KI + ROUNDS * 64:(i + 1) * KI, :] = jnp.zeros((64, NG * LANES), BF16)
        for _, _, m_ref, _, _, f_ref in sets:
            f_ref[i, STA * 8:(STA + 1) * 8, :] = zero
            m_ref[i, 0:2 * PITCH, :] = jnp.zeros((2 * PITCH, LANES), F32)

    def prepare(g, refs):
        t_ref, s_ref, m_ref, e_ref, d_ref, _ = refs
        low_rows = lane_iota((ROWS, LANES)) < 64
        before = [jnp.zeros((ROWS, LANES), F32)] * 2
        turned_before = jnp.zeros((ROWS, LANES), F32)
        for b in range(PLANE):
            piece = own_ref[b * NG + g, 0:ROWS, :].astype(F32)
            turned = pltpu.roll(piece, 64, 1)
            total = piece + turned
            mixed = jnp.where(low_rows, piece - turned, total)
            shared = jnp.where(low_rows, before[0], before[1])
            for s in range(STA):
                rows = slice(s * WIN, (s + 1) * WIN)
                own_rows = slice(b * PITCH, b * PITCH + WIN)
                t_ref[s, own_rows, :] = turned[rows]
                s_ref[s, own_rows, :] = total[rows]
                m_ref[s, (b + 2) * PITCH:(b + 2) * PITCH + WIN, :] = mixed[rows]
                e_ref[s, own_rows, :] = shared[rows]
                if s % 2 == 1:
                    d_ref[s // 2, own_rows, :] = jnp.where(
                        low_rows[:WIN], piece[rows], turned[(s + 1) * WIN:(s + 2) * WIN])
            if b < 2:
                for s in range(STA):
                    there = pl.ds((b * NG + g) * PITCH, WIN)
                    edge_t_ref[s, there, :] = turned[s * WIN:(s + 1) * WIN]
                    edge_s_ref[s, there, :] = total[s * WIN:(s + 1) * WIN]
            if b == PLANE - 2:
                for half in range(2):
                    partner_rows(edge_m_ref, edge_d_ref, piece, turned, mixed, pl.ds((half * NG + g) * PITCH, WIN))
            before = [piece, turned_before]
            turned_before = turned

    def compute(g, refs):
        t_ref, s_ref, m_ref, e_ref, d_ref, f_ref = refs
        lanes = pl.ds(pl.multiple_of(g * LANES, LANES), LANES)

        def add(acc, key, w, v):
            acc[key] = v if w == 0 else acc[key] + v

        for group in ((0, 1), (2, 3), (4, 5), (6,)):
            k1, k23 = {}, {}
            for w in range(WIN):
                rows = pl.ds(w, 8, stride=PITCH)
                t = {i: t_ref[i, rows, :] for i in group}
                total = {i: s_ref[i, rows, :] for i in group}
                for i in group:
                    add(k23, (i, i), w, t[i] * t[i])
                for j in range(group[0] + 1, STA):
                    mixed = m_ref[j, pl.ds(2 * PITCH + w, 8, stride=PITCH), :]
                    for i in group:
                        if i < j:
                            add(k23, (i, j), w, t[i] * mixed)
                for n in range(group[0] // 2, 3 if group[0] < 6 else 0):
                    shared = d_ref[n, rows, :]
                    for i in group:
                        if i < 2 * n + 2:
                            add(k1, (i, n), w, total[i] * shared)
            for i in group:
                auto = k23[i, i]
                f_ref[i, i * 8:(i + 1) * 8, :] = jnp.where(low, auto + pltpu.roll(auto, 64, 1), 0.0)
            for (i, n), k in k1.items():
                for j, part in zip((2 * n + 1, 2 * n + 2), spread_of(k)):
                    if j > i:
                        value = part - k23[i, j]
                        f_ref[i, j * 8:(j + 1) * 8, :] = value
                        f_ref[j, i * 8:(i + 1) * 8, :] = jnp.where(low, value, -value)
        for i in range(STA):
            k1, k23 = {}, {}
            for w in range(WIN):
                rows = pl.ds(w, 8, stride=PITCH)
                t = t_ref[i, rows, :]
                total = s_ref[i, rows, :]
                for j in range(STA):
                    add(k23, (1, j), w, t * m_ref[j, pl.ds(PITCH + w, 8, stride=PITCH), :])
                    add(k23, (2, j), w, t * m_ref[j, rows, :])
                    add(k1, j, w, total * e_ref[j, rows, :])
            values = {(1, STA): zero, (2, STA): zero}
            for j in range(STA):
                for r, k in zip((1, 2), spread_of(k1[j])):
                    values[r, j] = k - k23[r, j]
            for r in (1, 2):
                for j in range(0, 8, 2):
                    pair = jnp.concatenate([values[r, j], values[r, j + 1]], axis=0).astype(BF16)
                    base = i * KI + (r * 8 + j) * 8
                    x_ref[base:base + 16, lanes] = pair
        for i in range(STA):
            x_ref[i * KI:i * KI + 64, lanes] = f_ref[i].astype(BF16)

    def per_shard(g, carry):
        prepare(g, sets[0])
        compute(g, sets[0])
        return carry

    lax.fori_loop(0, NG, per_shard, 0)
    total = jnp.dot(hot_ref[...], x_ref[...], preferred_element_type=F32)
    out_ref[...] = (total[:, 0:128] + total[:, 128:256]) + (total[:, 256:384] + total[:, 384:512])


def edge_kernel(after_ref, before_ref, part_ref, hot_ref, t_ref, s_ref, own_m_ref, own_d_ref, bins_ref, slot_ref, out_ref,
                m_ref, d_ref, after_t_ref, after_s_ref, x_ref, after_hot_ref):
    low_rows = lane_iota((ROWS, LANES)) < 64
    zero = jnp.zeros((8, LANES), F32)
    for g in range(NG):
        piece = before_ref[g].astype(F32)
        turned = pltpu.roll(piece, 64, 1)
        mixed = jnp.where(low_rows, piece - turned, piece + turned)
        for half in range(2):
            base = (half * NG + g) * PITCH
            partner_rows(m_ref, d_ref, piece, turned, mixed, slice(base, base + WIN))
        piece = after_ref[g, 0:ROWS, :].astype(F32)
        turned = pltpu.roll(piece, 64, 1)
        total = piece + turned
        for n in range(8):
            s, base = min(n, STA - 1), ((n % 2) * NG + g) * PITCH
            after_t_ref[n // 2, base:base + WIN, :] = turned[s * WIN:(s + 1) * WIN]
            after_s_ref[n // 2, base:base + WIN, :] = total[s * WIN:(s + 1) * WIN]

    two = edge_labels((after_ref[0, ROWS:MSG, :],) * 2, 2, 2)
    lane_1 = lane_iota((1, LANES))
    upper, second_half = lane_1 >= 64, lane_1 % 8 >= 4
    for p in (0, 2):
        lower_unit = jnp.where(second_half, two[2 * p + 1:2 * p + 2], two[2 * p:2 * p + 1])
        upper_unit = jnp.where(second_half, two[2 * p + 3:2 * p + 4], two[2 * p + 2:2 * p + 3])
        wanted = jnp.broadcast_to(jnp.where(upper, upper_unit, lower_unit).astype(BF16), (LANES, LANES))
        after_hot_ref[:, p * 64:p * 64 + LANES] = jnp.where(
            bins_ref[...] == wanted, jnp.ones((LANES, LANES), BF16), jnp.zeros((LANES, LANES), BF16))

    x_ref[3 * LANES + 64:4 * LANES, :] = jnp.zeros((64, LANES), BF16)
    for unit in range(STA + 4):
        here = unit < STA
        own_t, own_s, place = (t_ref, s_ref, unit) if here else (after_t_ref, after_s_ref, unit - STA)
        other_m, other_d = (m_ref, d_ref) if here else (own_m_ref, own_d_ref)
        k1, k23 = {}, {}
        for w in range(WIN):
            rows = pl.ds(w, 8, stride=PITCH)
            t = own_t[place, rows, :]
            total = own_s[place, rows, :]
            for j in range(STA):
                v = t * other_m[j, rows, :]
                k23[j] = v if w == 0 else k23[j] + v
            for n in range(4):
                v = total * other_d[n, rows, :]
                k1[n] = v if w == 0 else k1[n] + v
        base = (unit if here else unit + 1) * 64
        for n in range(4):
            lower, upper = spread_of(k1[n])
            values = [lower - k23[2 * n], upper - k23[2 * n + 1] if n < 3 else zero]
            x_ref[base + n * 16:base + (n + 1) * 16, :] = jnp.concatenate(values, axis=0).astype(BF16)
    total = part_ref[...] + jnp.dot(hot_ref[...], x_ref[0:4 * LANES, :], preferred_element_type=F32)
    total = total + jnp.dot(after_hot_ref[...], x_ref[4 * LANES:, :], preferred_element_type=F32)
    parts = []
    for _ in range(3):
        parts.append(total.astype(BF16))
        total = total - parts[-1].astype(F32)
    total = jnp.dot(slot_ref[...], jnp.concatenate(parts, axis=1), preferred_element_type=F32)
    total = (total[:, 0:128] + total[:, 128:256]) + total[:, 256:384]
    for w, tile in enumerate(chunk_transpose([total[k * 64:(k + 1) * 64, :] for k in range(CAP)])):
        out_ref[pl.ds(w, 64, stride=4), :] = tile


def finish_kernel(in_ref, out_ref, s_ref):
    total = in_ref[0]
    for z in range(1, 8):
        total = total + in_ref[z]
    s_ref[...] = total * (1.0 / 64.0)
    tiles = chunk_transpose([s_ref[pl.ds(m, 8, stride=4), :] for m in range(4)])
    for k in range(CAP):
        for t in range(8):
            out_ref[k:k + 1, t * LANES:(t + 1) * LANES] = tiles[k][t:t + 1, :]


def in_vmem(value):
    return pltpu.with_memory_space_constraint(value, pltpu.VMEM)


def on_device(spectra, pair_bins, owner_count, bin_order):
    vmem = pl.BlockSpec(memory_space=pltpu.VMEM)
    in_hbm = pl.BlockSpec(memory_space=pl.ANY)
    packed, counts, order = pl.pallas_call(
        pack_kernel,
        out_shape=(
            pltpu.VMEM((32, MSG, LANES), BF16),
            pltpu.VMEM((1, owner_count.shape[0]), jnp.int32),
            pltpu.VMEM((1, bin_order.shape[0]), jnp.int32),
        ),
        in_specs=[in_hbm] * 4,
        out_specs=(vmem,) * 3,
        scratch_shapes=[
            pltpu.VMEM((STA, WIN, 4096), BF16),
            pltpu.VMEM((ROUNDS, STA, STA), jnp.int32),
            pltpu.SemaphoreType.DMA((STA,)),
            pltpu.SemaphoreType.DMA((3,)),
        ],
        name="pack",
    )(
        jnp.transpose(spectra, (1, 0, 2)),
        jnp.transpose(pair_bins, (1, 0, 2)),
        owner_count.reshape(1, -1),
        bin_order.reshape(1, -1),
    )
    own = lax.all_to_all(packed, ("y", "c", "win"), 0, 0)
    count = lax.axis_size("z")
    before = lax.ppermute(own[28:32, :ROWS], "z", [(i, (i + 1) % count) for i in range(count)])
    after = lax.ppermute(own[0:4], "z", [((i + 1) % count, i) for i in range(count)])
    operand = pltpu.VMEM((STA, 8 * PITCH, LANES), F32)
    shared = pltpu.VMEM((4, 8 * PITCH, LANES), F32)
    between = pl.pallas_call(
        cross_kernel,
        out_shape=(
            pltpu.VMEM((LANES, LANES), F32),
            pltpu.VMEM((LANES, 4 * LANES), BF16),
            operand,
            operand,
            operand,
            shared,
            pltpu.VMEM((LANES, LANES), BF16),
            pltpu.VMEM((256, LANES), BF16),
        ),
        in_specs=[vmem] * 3,
        out_specs=(vmem,) * 8,
        scratch_shapes=[
            *(pltpu.VMEM((count, rows, LANES), F32)
              for count, rows in ((STA, 144), (STA, 144), (STA, 176), (STA, 144), (3, 144), (STA, 64))),
            pltpu.VMEM((STA * KI, NG * LANES), BF16),
            pltpu.VMEM((LANES, STA * KI), BF16),
        ],
        compiler_params=SMALL,
        name="cross",
    )(in_vmem(own), in_vmem(counts), in_vmem(order))
    send = pl.pallas_call(
        edge_kernel,
        out_shape=pltpu.VMEM((256, LANES), F32),
        in_specs=[vmem] * 10,
        out_specs=vmem,
        scratch_shapes=[
            operand,
            shared,
            shared,
            shared,
            pltpu.VMEM((6 * LANES, LANES), BF16),
            pltpu.VMEM((LANES, 2 * LANES), BF16),
        ],
        compiler_params=SMALL,
        name="edge",
    )(in_vmem(after), in_vmem(before), *(in_vmem(v) for v in between))
    got = lax.all_to_all(send.reshape(256, 1, LANES), ("z", "y", "c", "win"), 0, 0)
    got = in_vmem(got.reshape(8, 32, LANES))
    return pl.pallas_call(
        finish_kernel,
        out_shape=jax.ShapeDtypeStruct((CAP, 1024), F32),
        in_specs=[vmem],
        out_specs=vmem,
        scratch_shapes=[pltpu.VMEM((32, LANES), F32)],
        compiler_params=SMALL,
        name="finish",
    )(got)


def solution(mesh):
    fine = Mesh(mesh.devices.reshape(8, 4, 2, 4), ("z", "y", "c", "win"))
    sta = ("z", "y", "c")
    return jax.shard_map(
        on_device,
        mesh=fine,
        in_specs=(P("win", sta, None), P(sta, None, None), P(), P()),
        out_specs=P(sta, "win"),
        check_vma=False,
    )
```
